256 devices in a mesh: chain: 4 (over y), block: 64 (over x, z, core).
Axes of the slice: x: 4, y: 4, z: 8, core: 2. Of those that a mesh axis runs over, the one named last changes fastest.
Arguments:
- site_blocks: bfloat16 [4, 4, 8192, 2, 128], P('chain', None, 'block'), may hold values from -0.5 to 0.5
- left_carry: bfloat16 [4, 8192, 5, 128], P(None, 'block'), may hold values from -6 to 6
- mpo: float32 [4, 5, 5, 2, 2], replicated, may hold values from -3 to 3
- sketch: bfloat16 [4, 64, 640, 128], P('chain', 'block'), may hold values from -0.25 to 0.25
- ranks: int32 [4, 64], P(None, 'block'), may hold values from 32 to 128, as said below
Outputs:
- new_sites: bfloat16 [4, 4, 8192, 2, 128], P('chain', None, 'block')
- carries: bfloat16 [4, 4, 8192, 5, 128], P('chain', None, 'block')
The draws below stay inside these ranges and needn't reach their ends.
Inputs may be any that keep to these rules, and one draw needn't show every extreme that they name: Every site has the same ranks; sector 0 keeps 128 // 4 to 64 columns, the top sector 64 - 1 keeps all 128, every other sector 128 // 2 or more.
All inputs are finite; a program needn't handle non-finite values.
Results may differ from the reference program's by a relative error of at most 0.03.
Values may be sent and summed in bfloat16 or wider, within the bound.
A program may use at most 64 MiB of HBM per device.

```python
import jax
import jax.numpy as jnp
from jax import lax

DS = 128
WB = 5
PHYS = 2
STATES = 4
SITES = 4
NB = 64
D = 8192


def draw_ranks(key, part):
    drawn_ranks = jax.random.randint(key, (1, NB), DS // 2, DS + 1, dtype=jnp.int32)
    edge_ranks = jax.random.randint(jax.random.fold_in(key, 7), (1, 1), DS // 4, DS // 2 + 1, dtype=jnp.int32)
    sector_ids = jnp.arange(NB, dtype=jnp.int32)[None, :]
    kept_counts = jnp.where(sector_ids == 0, edge_ranks, drawn_ranks)
    kept_counts = jnp.where(sector_ids == NB - 1, DS, kept_counts).astype(jnp.int32)
    return jnp.broadcast_to(kept_counts, (SITES, NB)).astype(jnp.int32)


def level_of(stream_key, extent, split, least, top_value):
    loudness = 1.0
    for position, blocks in split:
        draws = jax.random.uniform(jax.random.fold_in(jax.random.fold_in(stream_key, 6), position), (blocks,), jnp.float32, least / len(split), top_value / len(split))
        loudness = loudness * jnp.repeat(jnp.exp(draws), extent[position] // blocks).reshape((-1,) + (1,) * (len(extent) - 1 - position))
    return loudness


def noise(own_key, shape, spread, limit, cuts=(), kind=jnp.bfloat16):
    loudness = level_of(own_key, shape, cuts, -0.22, 0.18) if cuts else 1.0
    drawn = jax.random.normal(own_key, shape, jnp.float32) * spread * loudness
    return jnp.minimum(jnp.maximum(drawn, -limit), limit).astype(kind)


def setup_inputs(seed: int = 0) -> dict:
    key_list = jax.random.split(jax.random.key(seed), 6)
    site_blocks = noise(key_list[0], (SITES, STATES, D, PHYS, DS), DS ** -0.5, 0.5, ((0, 4), (2, 64)))
    left_carry = noise(key_list[1], (STATES, D, WB, DS), 1.0, 6.0, ((1, 64),))
    mpo = noise(key_list[2], (SITES, WB, WB, PHYS, PHYS), 0.5, 3.0, (), jnp.float32)
    sketch = noise(key_list[3], (SITES, NB, WB * DS, DS), (WB * DS) ** -0.5, 0.25, ((0, 4), (1, 64)))
    ranks = draw_ranks(jax.random.fold_in(key_list[5], 71), 0)
    return {"site_blocks": site_blocks, "left_carry": left_carry, "mpo": mpo, "sketch": sketch, "ranks": ranks}


CHARGES = (0, 1, -1, 0, 0)

def rule_mask():
    charges = jnp.array(CHARGES, dtype=jnp.int32)
    physical = jnp.arange(2, dtype=jnp.int32)
    state_change = physical[None, None, :, None] - physical[None, None, None, :]
    charge_change = charges[None, :, None, None] - charges[:, None, None, None]
    return (state_change == charge_change).astype(jnp.float32)

def move_sectors(values, offset):
    if offset == 0:
        return values
    empty = jnp.zeros_like(values[:, :1])
    if offset == 1:
        return jnp.concatenate([empty, values[:, :-1]], axis=1)
    return jnp.concatenate([values[:, 1:], empty], axis=1)

def solve_lower(factor, right_side):
    return jax.scipy.linalg.solve_triangular(factor, right_side.T, lower=True)

def reference(site_blocks, left_carry, mpo, sketch, ranks):
    selection = rule_mask()
    carried = left_carry.reshape(STATES, NB, DS, WB, DS)
    sector_ids = jnp.arange(NB, dtype=jnp.int32)
    top_mask = jnp.logical_or(sector_ids[:, None] < NB - 1, jnp.arange(2, dtype=jnp.int32)[None, :] == 0)
    top_mask = top_mask.astype(jnp.bfloat16)[None, :, None, :, None]
    column_ids = jnp.arange(DS, dtype=jnp.int32)
    column_count = WB * DS
    ridge_value = DS / 4.0
    sites_out = []
    carries_out = []
    for site_no in range(SITES):
        blocks = site_blocks[site_no].reshape(STATES, NB, DS, 2, DS) * top_mask
        coupled = mpo[site_no] * selection
        contracted = jnp.zeros((STATES, NB, 2, DS, WB, DS), jnp.float32)
        for channel in range(WB):
            selected = move_sectors(blocks, CHARGES[channel]).astype(jnp.float32)
            products = jnp.einsum('anij,anjsk->ansik', carried[:, :, :, channel, :].astype(jnp.float32), selected, precision=lax.Precision.HIGHEST)
            contracted = contracted + jnp.einsum('vts,ansik->antivk', coupled[channel], products, precision=lax.Precision.HIGHEST)
        contracted = contracted.astype(jnp.bfloat16)
        from_below = move_sectors(contracted[:, :, 1], 1)
        stacked = jnp.concatenate([contracted[:, :, 0].reshape(STATES, NB, DS, column_count), from_below.reshape(STATES, NB, DS, column_count)], axis=2)
        sketched = jnp.einsum('anrc,ncj->anrj', stacked.astype(jnp.float32), sketch[site_no].astype(jnp.float32), precision=lax.Precision.HIGHEST)
        kept_cols = (column_ids[None, :] < ranks[site_no][:, None]).astype(jnp.float32)
        sketched = sketched * kept_cols[None, :, None, :]
        gram_matrix = jnp.einsum('anrj,anrl->anjl', sketched, sketched, precision=lax.Precision.HIGHEST)
        diag_terms = ridge_value * kept_cols + (1.0 - kept_cols)
        gram_matrix = gram_matrix + jnp.eye(DS, dtype=jnp.float32)[None, None] * diag_terms[None, :, None, :]
        factor = jnp.linalg.cholesky(gram_matrix)
        isometry = jax.vmap(jax.vmap(solve_lower))(factor, sketched).astype(jnp.bfloat16)
        carried = jnp.einsum('anlr,anrc->anlc', isometry.astype(jnp.float32), stacked.astype(jnp.float32), precision=lax.Precision.HIGHEST).astype(jnp.bfloat16).reshape(STATES, NB, DS, WB, DS)
        sites_out.append(isometry.reshape(STATES, NB * DS, 2, DS))
        carries_out.append(carried.reshape(STATES, NB * DS, WB, DS))
    return (jnp.stack(sites_out), jnp.stack(carries_out))
```

```python
import functools

import jax
import jax.numpy as jnp
from jax import lax
from jax.experimental import pallas as pl
from jax.experimental.pallas import tpu as pltpu
from jax.sharding import PartitionSpec as P

CHARGES = (0, 1, -1, 0, 0)
WB = len(CHARGES)
DS = 128
ROWS = 8
MESH = pl.DeviceIdType.MESH
F32 = jnp.float32
BF16 = jnp.bfloat16
NN = (((1,), (0,)), ((), ()))
NT = (((1,), (1,)), ((), ()))


def dot(a, b, dims=NN):
    return lax.dot_general(a, b, dims, preferred_element_type=F32)


def halves(x):
    high = x.astype(BF16)
    return high, (x - high.astype(F32)).astype(BF16)


def wide(v, width):
    return v if width == v.shape[1] else jnp.concatenate([v] * (width // v.shape[1]), axis=1)


def invert_factor(work, inverse):
    width = work.shape[1]

    def block(step, carry):
        first = pl.multiple_of(step * ROWS, ROWS)
        shift = lax.rem(DS - first, DS)
        rows = work[pl.ds(first, ROWS), :]
        turned = pltpu.roll(work[:, :DS], shift, axis=1)
        corner = pltpu.roll(rows[:, :DS], shift, axis=1)
        columns = [jnp.broadcast_to(turned[:, c : c + 1], (DS, DS)) for c in range(ROWS)]
        tops = [jnp.broadcast_to(corner[:, c : c + 1], (ROWS, DS)) for c in range(ROWS)]
        low = [
            [jnp.broadcast_to(tops[c][r : r + 1, :], (ROWS, DS)) if r >= c else None for c in range(ROWS)]
            for r in range(ROWS)
        ]
        scale = []
        for c in range(ROWS):
            scale.append(lax.rsqrt(low[c][c]))
            for r in range(c + 1, ROWS):
                low[r][c] = low[r][c] * scale[c]
            for q in range(c + 1, ROWS):
                for r in range(q, ROWS):
                    low[r][q] = low[r][q] - low[r][c] * low[q][c]
        upper = []
        for c in range(ROWS):
            x = jnp.broadcast_to(rows[c : c + 1, :], (ROWS, width))
            for q in range(c):
                x = x - wide(low[c][q], width) * upper[q]
            upper.append(x * wide(scale[c], width))
        inverse[pl.ds(first, ROWS), :] = jnp.concatenate([u[0:1, DS:] for u in upper], axis=0)
        solved = [None] * ROWS
        for c in reversed(range(ROWS)):
            x = upper[c]
            for q in range(c + 1, ROWS):
                x = x - wide(low[q][c], width) * solved[q]
            solved[c] = x * wide(scale[c], width)
        for i in range(DS // ROWS):
            part = pl.ds(i * ROWS, ROWS)
            rest = work[part, :]
            for c in range(ROWS):
                rest = rest - wide(columns[c][i * ROWS : (i + 1) * ROWS, :], width) * solved[c]
            work[part, :] = rest
        return carry

    lax.fori_loop(0, DS // ROWS, block, 0)


def kernel(
    sites, sectors,
    mpo, ranks, blocks_in, carry_in, sketch_in,
    sites_out, carry_out,
    blk, sk, car, terms, sent, below, y_out, y_in, iso, coupled, sketched, plain, work, inverse,
    first_sem, blk_sem, sk_sem, pass_sem, load_sem, y_send, y_recv, t_send, t_recv, o_send, o_recv,
):
    c = lax.axis_index("chain")
    p = lax.axis_index("block")
    up = {"block": lax.rem(p + 1, sectors)}
    down = {"block": lax.rem(p + sectors - 1, sectors)}

    def remote(src, dst, send, recv, to):
        return pltpu.make_async_remote_copy(
            src_ref=src, dst_ref=dst, send_sem=send, recv_sem=recv, device_id=to, device_id_type=MESH
        )

    local_carry = pltpu.make_async_copy(carry_in.at[c], car.at[0], load_sem)
    local_block = pltpu.make_async_copy(blocks_in.at[c], blk.at[c, 0], blk_sem.at[c, 0])
    local_sketch = pltpu.make_async_copy(sketch_in, sk.at[c, 0], sk_sem.at[c, 0])
    local_block.start()
    local_sketch.start()
    local_carry.start()

    barrier = pltpu.get_barrier_semaphore()
    for d in range(1, sites):
        pl.semaphore_signal(barrier, inc=1, device_id={"chain": lax.rem(c + d, sites)}, device_id_type=MESH)
    pl.semaphore_signal(barrier, inc=1, device_id=up, device_id_type=MESH)
    pl.semaphore_signal(barrier, inc=1, device_id=down, device_id_type=MESH)
    pl.semaphore_wait(barrier, sites + 1)

    def share(d, which):
        peer = lax.rem(c + d, sites)
        to = {"chain": peer}
        if which == 0:
            return remote(blocks_in.at[peer], blk.at[c, 0], first_sem.at[0, d], blk_sem.at[c, 0], to)
        return remote(sketch_in, sk.at[c, 0], first_sem.at[1, d], sk_sem.at[c, 0], to)

    def send_shares():
        for which in range(2):
            for d in range(1, sites):
                share(d, which).start()

    def passed(k, which):
        if which == 0:
            return remote(blk.at[k, 0], blk.at[k, 1], pass_sem.at[k, 0], blk_sem.at[k, 1], up)
        if which == 1:
            return remote(blk.at[k, 0], blk.at[k, 2], pass_sem.at[k, 1], blk_sem.at[k, 2], down)
        return remote(sk.at[k, 0], sk.at[k, 1], pass_sem.at[k, 2], sk_sem.at[k, 1], down)

    def pass_on(k):
        pltpu.make_async_copy(blk.at[k, 0], blk.at[k, 0], blk_sem.at[k, 0]).wait()
        passed(k, 0).start()
        passed(k, 1).start()
        pltpu.make_async_copy(sk.at[k, 0], sk.at[k, 0], sk_sem.at[k, 0]).wait()
        passed(k, 2).start()

    top = (p < sectors - 1).astype(F32)
    below_top = (p < sectors - 2).astype(F32)
    bottom = (p > 0).astype(F32)

    def prepare(k):
        passed(k, 0).wait_recv()
        passed(k, 1).wait_recv()
        for w in range(WB):
            where = {0: 0, 1: 1, -1: 2}[CHARGES[w]]
            if w < 3:
                plain[...] = blk[k, where].astype(F32)
                own = [plain[pl.ds(s, DS, stride=2), :] for s in range(2)]
                if w == 0:
                    centre = own
            else:
                own = centre
            for v in range(WB):
                for t in range(2):
                    s = t - CHARGES[v] + CHARGES[w]
                    if s not in (0, 1):
                        continue
                    weight = mpo[k, w, t, s, v]
                    if where == 0 and s == 1:
                        weight = weight * top
                    elif where == 1:
                        weight = weight * bottom
                    elif where == 2:
                        weight = weight * (top if s == 0 else below_top)
                    coupled[t, pl.ds(w * DS, DS), pl.ds(v * DS, DS)] = (own[s] * weight).astype(BF16)
        passed(k, 2).wait_recv()
        for t in range(2):
            product = dot(coupled[t], sk[k, t])
            for w in range(WB):
                sketched[pl.ds(t * DS, DS), pl.ds(w * DS, DS)] = product[w * DS : (w + 1) * DS, :].T.astype(BF16)

    @pl.when(c == 0)
    def _():
        send_shares()

    coupled[...] = jnp.zeros_like(coupled)
    pass_on(0)

    @pl.when(c > 0)
    def _():
        send_shares()

    prepare(0)
    local_carry.wait()

    def output(k, which):
        return (iso.at[k], sites_out.at[c]) if which == 0 else (car.at[k + 1], carry_out.at[c])

    def outgoing(k, which):
        return remote(*output(k, which), o_send.at[k, which], o_recv.at[c, which], {"chain": k})

    def kept(k, which):
        return pltpu.make_async_copy(*output(k, which), o_send.at[k, which])

    def deliver(k, which):
        @pl.when(c == k)
        def _():
            kept(k, which).start()

        @pl.when(c != k)
        def _():
            outgoing(k, which).start()

    row_ids = lax.broadcasted_iota(jnp.int32, (DS, DS), 0)
    column_ids = lax.broadcasted_iota(jnp.int32, (DS, DS), 1)

    def step(k, carry):
        carried = jnp.concatenate([car[k, w] for w in range(WB)], axis=1)
        y = dot(sketched[...], carried, NT)
        y_out[k] = y[DS:]
        y_copy = remote(y_out.at[k], y_in.at[k], y_send.at[k], y_recv.at[k], up)
        y_copy.start()
        sent[k] = dot(carried, coupled[1]).astype(BF16)
        t_copy = remote(sent.at[k], below.at[k], t_send.at[k], t_recv.at[k], up)
        t_copy.start()
        terms[...] = dot(carried, coupled[0]).astype(BF16)

        @pl.when(k + 1 < sites)
        def _():
            pass_on(k + 1)

        rank = ranks[0, k]
        upper_rank = jnp.where(p > 0, rank, 0)
        y_copy.wait_recv()
        y0 = jnp.where(row_ids < rank, y[:DS], 0.0)
        y1 = jnp.where(row_ids < upper_rank, y_in[k], 0.0)
        high, low = halves(jnp.concatenate([y0, y1], axis=1))
        gram = dot(
            jnp.concatenate([high, high, low], axis=1), jnp.concatenate([high, low, high], axis=1), NT
        )
        ridge = jnp.where(row_ids < rank, DS / 4.0, 1.0)
        work[:, :DS] = gram + jnp.where(row_ids == column_ids, ridge, 0.0)
        work[:, DS:] = jnp.where(row_ids == column_ids, 1.0, 0.0)
        invert_factor(work, inverse)
        inv_high, inv_low = halves(inverse[...])
        frame = dot(
            jnp.concatenate([inv_high, inv_low, inv_high], axis=1),
            jnp.concatenate([high, high, low], axis=0),
        )
        plain[pl.ds(0, DS, stride=2), :] = frame[:, :DS]
        plain[pl.ds(1, DS, stride=2), :] = frame[:, DS:]
        iso[k] = plain[...].astype(BF16)
        deliver(k, 0)
        t_copy.wait_recv()
        new = dot(frame.astype(BF16), jnp.concatenate([terms[...], below[k]], axis=0)).astype(BF16)
        for v in range(WB):
            car[k + 1, v] = new[:, v * DS : (v + 1) * DS]
        deliver(k, 1)

        @pl.when(k + 1 < sites)
        def _():
            prepare(k + 1)

        y_copy.wait_send()
        t_copy.wait_send()
        return carry

    lax.fori_loop(0, sites, step, 0)

    for d in range(1, sites):
        for which in range(2):
            share(d, which).wait_send()
    for k in range(sites):
        for which in range(3):
            passed(k, which).wait_send()

        @pl.when(c == k)
        def _():
            for which in range(2):
                kept(k, which).wait()

        @pl.when(c != k)
        def _():
            for which in range(2):
                outgoing(k, which).wait_send()

    for d in range(1, sites):
        peer = lax.rem(c + d, sites)
        remote(iso.at[0], sites_out.at[peer], o_send.at[0, 0], o_recv.at[peer, 0], {"chain": peer}).wait_recv()
        remote(car.at[1], carry_out.at[peer], o_send.at[0, 1], o_recv.at[peer, 1], {"chain": peer}).wait_recv()


def per_device(site_blocks, left_carry, mpo, sketch, ranks):
    sites = lax.axis_size("chain")
    sectors = lax.axis_size("block")
    states = left_carry.shape[0]
    dma = pltpu.SemaphoreType.DMA
    vmem = pltpu.VMEM
    new_sites, carries = pl.pallas_call(
        functools.partial(kernel, sites, sectors),
        name="zip_up",
        out_shape=(
            jax.ShapeDtypeStruct((states, 2 * DS, DS), BF16),
            jax.ShapeDtypeStruct((states, WB, DS, DS), BF16),
        ),
        in_specs=[
            pl.BlockSpec(memory_space=pltpu.SMEM),
            pl.BlockSpec(memory_space=pltpu.SMEM),
            pl.BlockSpec(memory_space=pl.ANY),
            pl.BlockSpec(memory_space=pl.ANY),
            pl.BlockSpec(memory_space=pl.ANY),
        ],
        out_specs=(pl.BlockSpec(memory_space=pl.ANY), pl.BlockSpec(memory_space=pl.ANY)),
        scratch_shapes=[
            vmem((sites, 3, 2 * DS, DS), BF16),
            vmem((sites, 2, WB * DS, DS), BF16),
            vmem((sites + 1, WB, DS, DS), BF16),
            vmem((DS, WB * DS), BF16),
            vmem((sites, DS, WB * DS), BF16),
            vmem((sites, DS, WB * DS), BF16),
            vmem((sites, DS, DS), F32),
            vmem((sites, DS, DS), F32),
            vmem((sites, 2 * DS, DS), BF16),
            vmem((2, WB * DS, WB * DS), BF16),
            vmem((2 * DS, WB * DS), BF16),
            vmem((2 * DS, DS), F32),
            vmem((DS, 2 * DS), F32),
            vmem((DS, DS), F32),
            dma((2, sites)),
            dma((sites, 3)),
            dma((sites, 2)),
            dma((sites, 3)),
            dma,
            dma((sites,)),
            dma((sites,)),
            dma((sites,)),
            dma((sites,)),
            dma((sites, 2)),
            dma((sites, 2)),
        ],
        compiler_params=pltpu.CompilerParams(
            collective_id=0, has_side_effects=True, vmem_limit_bytes=40 * 2**20
        ),
    )(
        jnp.transpose(mpo, (0, 1, 3, 4, 2)),
        jnp.transpose(ranks),
        site_blocks.reshape(states, 2 * DS, DS),
        jnp.transpose(left_carry, (0, 2, 1, 3)),
        sketch.reshape(WB * DS, DS),
    )
    return (
        new_sites.reshape(1, states, DS, 2, DS),
        jnp.transpose(carries, (0, 2, 1, 3))[None],
    )


def solution(mesh):
    return jax.shard_map(
        per_device,
        mesh=mesh,
        in_specs=(
            P("chain", None, "block", None, None),
            P(None, "block", None, None),
            P(),
            P("chain", "block", None, None),
            P(None, "block"),
        ),
        out_specs=(P("chain", None, "block", None, None), P("chain", None, "block", None, None)),
        check_vma=False,
    )
```

```python
import functools

import jax
import jax.numpy as jnp
from jax import lax
from jax.experimental import pallas as pl
from jax.experimental.pallas import tpu as pltpu
from jax.sharding import PartitionSpec as P

CHARGES = (0, 1, -1, 0, 0)
WB = len(CHARGES)
DS = 128
ROWS = 8
MESH = pl.DeviceIdType.MESH
F32 = jnp.float32
BF16 = jnp.bfloat16
NN = (((1,), (0,)), ((), ()))
NT = (((1,), (1,)), ((), ()))


def dot(a, b, dims=NN):
    return lax.dot_general(a, b, dims, preferred_element_type=F32)


def halves(x):
    high = x.astype(BF16)
    return high, (x - high.astype(F32)).astype(BF16)


def wide(v, width):
    return v if width == v.shape[1] else jnp.concatenate([v] * (width // v.shape[1]), axis=1)


def invert_factor(work, inverse):
    width = work.shape[1]
    count = DS // ROWS
    part = [slice(i * ROWS, (i + 1) * ROWS) for i in range(count)]

    def lanes(x, first):
        return [jnp.broadcast_to(x[:, first + q : first + q + 1], (ROWS, DS)) for q in range(ROWS)]

    def entry(columns, r, q):
        return jnp.broadcast_to(columns[q][r : r + 1, :], (ROWS, DS))

    rows = work[part[0], :]
    corner = lanes(rows, 0)
    for block in range(count):
        first = block * ROWS
        low = [[entry(corner, r, q) if r >= q else None for q in range(ROWS)] for r in range(ROWS)]
        scale = []
        for q in range(0, ROWS, 2):
            e = q + 1
            inv = lax.rsqrt(low[q][q])
            det = low[q][q] * low[e][e] - low[e][q] * low[e][q]
            inv_e = lax.rsqrt(det) * (low[q][q] * inv)
            scale += [inv, inv_e]
            for r in range(e, ROWS):
                low[r][q] = low[r][q] * inv
            for r in range(e + 1, ROWS):
                low[r][e] = (low[r][e] - low[r][q] * low[e][q]) * inv_e
            for n in range(e + 1, ROWS):
                for r in range(n, ROWS):
                    low[r][n] = low[r][n] - (low[r][q] * low[n][q] + low[r][e] * low[n][e])
        upper = []
        for q in range(ROWS):
            x = jnp.broadcast_to(rows[q : q + 1, :], (ROWS, width))
            for n in range(q):
                x = x - wide(low[q][n], width) * upper[n]
            upper.append(x * wide(scale[q], width))
        for q in range(ROWS):
            inverse[first + q : first + q + 1, :] = upper[q][0:1, DS:]
        if block + 1 == count:
            break
        below = work[part[block + 1], :]
        left = []
        for q, x in enumerate(lanes(below, first)):
            for n in range(q):
                x = x - left[n] * low[q][n]
            left.append(x * scale[q])
        corner = lanes(below, first + ROWS)
        for q in range(ROWS):
            for n in range(ROWS):
                corner[q] = corner[q] - left[n] * jnp.broadcast_to(left[n][q : q + 1, :], (ROWS, DS))
        rows = below
        for q in range(ROWS):
            rows = rows - wide(left[q], width) * upper[q]
        solved = [None] * ROWS
        for q in reversed(range(ROWS)):
            x = upper[q]
            for n in range(q + 1, ROWS):
                x = x - wide(low[n][q], width) * solved[n]
            solved[q] = x * wide(scale[q], width)
        for i in range(block + 2, count):
            rest = work[part[i], :]
            columns = lanes(rest, first)
            for q in range(ROWS):
                rest = rest - wide(columns[q], width) * solved[q]
            work[part[i], :] = rest


def kernel(
    sites, sectors,
    mpo_in, ranks_in, blocks_in, carry_in, sketch_in,
    sites_out, carry_out,
    mpo, ranks, blk, sk, car, sent, below, iso, coupled, plain, work, inverse,
    share_sem, blk_sem, sk_sem, pass_sem, load_sem, t_send, t_recv, o_send, o_recv,
):
    c = lax.axis_index("chain")
    p = lax.axis_index("block")
    up = {"block": lax.rem(p + 1, sectors)}
    down = {"block": lax.rem(p + sectors - 1, sectors)}

    def remote(src, dst, send, recv, to):
        return pltpu.make_async_remote_copy(
            src_ref=src, dst_ref=dst, send_sem=send, recv_sem=recv, device_id=to, device_id_type=MESH
        )

    loads = (
        pltpu.make_async_copy(mpo_in, mpo, load_sem.at[0]),
        pltpu.make_async_copy(ranks_in, ranks, load_sem.at[1]),
        pltpu.make_async_copy(carry_in.at[c], car.at[0], load_sem.at[2]),
    )
    pltpu.make_async_copy(blocks_in.at[c], blk.at[c, 0], blk_sem.at[c, 0]).start()
    pltpu.make_async_copy(sketch_in, sk.at[c], sk_sem.at[c]).start()
    for load in loads:
        load.start()

    barrier = pltpu.get_barrier_semaphore()
    for d in range(1, sites):
        pl.semaphore_signal(barrier, inc=1, device_id={"chain": lax.rem(c + d, sites)}, device_id_type=MESH)
    pl.semaphore_signal(barrier, inc=1, device_id=up, device_id_type=MESH)
    pl.semaphore_signal(barrier, inc=1, device_id=down, device_id_type=MESH)
    pl.semaphore_wait(barrier, sites + 1)

    def share(d, which):
        peer = lax.rem(c + d, sites)
        to = {"chain": peer}
        if which == 0:
            return remote(blocks_in.at[peer], blk.at[c, 0], share_sem.at[0, d], blk_sem.at[c, 0], to)
        return remote(sketch_in, sk.at[c], share_sem.at[1, d], sk_sem.at[c], to)

    def passed(k, which, src):
        to = up if which == 0 else down
        return remote(src, blk.at[k, which + 1], pass_sem.at[k, which], blk_sem.at[k, which + 1], to)

    ORDER = (1, sites - 1) + tuple(range(2, sites - 1))

    def share_blocks():
        for d in ORDER:
            share(d, 0).start()
        for which in range(2):
            passed(c, which, blocks_in.at[c]).start()

    def share_sketch():
        for d in ORDER:
            share(d, 1).start()

    def arrived(ref, sem):
        pltpu.make_async_copy(ref, ref, sem).wait()

    def pass_on(k):
        arrived(blk.at[k, 0], blk_sem.at[k, 0])

        @pl.when(c != k)
        def _():
            for which in range(2):
                passed(k, which, blk.at[k, 0]).start()

    top = (p < sectors - 1).astype(F32)
    below_top = (p < sectors - 2).astype(F32)
    bottom = (p > 0).astype(F32)

    def prepare(k):
        for w in range(WB):
            where = {0: 0, 1: 1, -1: 2}[CHARGES[w]]
            if w < 3:
                if where:
                    arrived(blk.at[k, where], blk_sem.at[k, where])
                plain[w] = blk[k, where].astype(F32)
            own = [plain[where, pl.ds(s, DS, stride=2), :] for s in range(2)]
            for v in range(WB):
                for t in range(2):
                    s = t - CHARGES[v] + CHARGES[w]
                    if s not in (0, 1):
                        continue
                    weight = mpo[k, w, t, s : s + 1, v : v + 1]
                    if where == 0 and s == 1:
                        weight = weight * top
                    elif where == 1:
                        weight = weight * bottom
                    elif where == 2:
                        weight = weight * (top if s == 0 else below_top)
                    coupled[t, pl.ds(w * DS, DS), pl.ds(v * DS, DS)] = (own[s] * weight).astype(BF16)

    share_blocks()

    @pl.when(c == 0)
    def _():
        share_sketch()

    for t in range(2):
        for w in range(WB):
            for v in range(WB):
                if t - CHARGES[v] + CHARGES[w] not in (0, 1):
                    coupled[t, pl.ds(w * DS, DS), pl.ds(v * DS, DS)] = jnp.zeros((DS, DS), BF16)
    for load in loads:
        load.wait()
    pass_on(0)
    prepare(0)

    def output(k, which):
        return (iso.at[k], sites_out.at[c]) if which == 0 else (car.at[k + 1], carry_out.at[c])

    def outgoing(k, which):
        return remote(*output(k, which), o_send.at[k, which], o_recv.at[c, which], {"chain": k})

    def kept(k, which):
        return pltpu.make_async_copy(*output(k, which), o_send.at[k, which])

    def deliver(k, which):
        @pl.when(c == k)
        def _():
            kept(k, which).start()

        @pl.when(c != k)
        def _():
            outgoing(k, which).start()

    row_ids = lax.broadcasted_iota(jnp.int32, (DS, DS), 0)
    column_ids = lax.broadcasted_iota(jnp.int32, (DS, DS), 1)
    rows_f = row_ids.astype(F32)
    site_ids = lax.broadcasted_iota(jnp.int32, (1, sites), 1)
    CUTS = ((0, 3), (3, WB))

    def raised(k, part):
        v0, v1 = CUTS[part]
        cut = pl.ds(v0, v1 - v0)
        return remote(sent.at[k, cut], below.at[k, cut], t_send.at[k, part], t_recv.at[k, part], up)

    def step(k, carry):
        carried = jnp.concatenate([car[k, w] for w in range(WB)], axis=1)
        for part, (v0, v1) in enumerate(CUTS):
            rows = dot(carried, coupled[1, :, pl.ds(v0 * DS, (v1 - v0) * DS)]).astype(BF16)
            for v in range(v0, v1):
                sent[k, v] = rows[:, (v - v0) * DS : (v - v0 + 1) * DS]
            raised(k, part).start()
        terms = dot(carried, coupled[0]).astype(BF16)
        arrived(sk.at[k], sk_sem.at[k])
        tests = sk[k].T
        rank = jnp.sum(jnp.where(site_ids == k, ranks[...].astype(F32), 0.0), axis=1, keepdims=True)
        upper_rank = rank * bottom
        y0 = jnp.where(rows_f < rank, dot(tests, terms, NT), 0.0)

        @pl.when(k == 0)
        def _():
            for later in range(1, sites):
                pass_on(later)

        @pl.when(jnp.logical_and(k == 0, c > 0))
        def _():
            share_sketch()

        for part in range(len(CUTS)):
            raised(k, part).wait_recv()
        lower = jnp.concatenate([below[k, v] for v in range(WB)], axis=1)
        y1 = jnp.where(rows_f < upper_rank, dot(tests, lower, NT), 0.0)
        high, low = halves(jnp.concatenate([y0, y1], axis=1))
        gram = dot(
            jnp.concatenate([high, high, low], axis=1), jnp.concatenate([high, low, high], axis=1), NT
        )
        ridge = jnp.where(rows_f < rank, DS / 4.0, 1.0)
        work[:, :DS] = gram + jnp.where(row_ids == column_ids, ridge, 0.0)
        work[:, DS:] = jnp.where(row_ids == column_ids, 1.0, 0.0)
        invert_factor(work, inverse)

        inv_high, inv_low = halves(inverse[...])
        frame = dot(
            jnp.concatenate([inv_high, inv_low, inv_high], axis=1),
            jnp.concatenate([high, high, low], axis=0),
        )
        new = dot(frame.astype(BF16), jnp.concatenate([terms, lower], axis=0)).astype(BF16)
        for v in range(WB):
            car[k + 1, v] = new[:, v * DS : (v + 1) * DS]
        deliver(k, 1)
        plain[0, pl.ds(0, DS, stride=2), :] = frame[:, :DS]
        plain[0, pl.ds(1, DS, stride=2), :] = frame[:, DS:]
        iso[k] = plain[0].astype(BF16)
        deliver(k, 0)

        @pl.when(k + 1 < sites)
        def _():
            prepare(k + 1)

        return carry

    lax.fori_loop(0, sites, step, 0)

    for d in range(1, sites):
        for which in range(2):
            share(d, which).wait_send()
    for k in range(sites):
        for part in range(2):
            passed(k, part, blk.at[k, 0]).wait_send()
            raised(k, part).wait_send()

        @pl.when(c == k)
        def _():
            for which in range(2):
                kept(k, which).wait()

        @pl.when(c != k)
        def _():
            for which in range(2):
                outgoing(k, which).wait_send()

    for d in range(1, sites):
        peer = lax.rem(c + d, sites)
        remote(iso.at[0], sites_out.at[peer], o_send.at[0, 0], o_recv.at[peer, 0], {"chain": peer}).wait_recv()
        remote(car.at[1], carry_out.at[peer], o_send.at[0, 1], o_recv.at[peer, 1], {"chain": peer}).wait_recv()


def per_device(site_blocks, left_carry, mpo, sketch, ranks):
    sites = lax.axis_size("chain")
    sectors = lax.axis_size("block")
    states = left_carry.shape[0]
    dma = pltpu.SemaphoreType.DMA
    vmem = pltpu.VMEM
    new_sites, carries = pl.pallas_call(
        functools.partial(kernel, sites, sectors),
        name="zip_up",
        out_shape=(
            jax.ShapeDtypeStruct((states, 2 * DS, DS), BF16),
            jax.ShapeDtypeStruct((states, WB, DS, DS), BF16),
        ),
        in_specs=[
            pl.BlockSpec(memory_space=pltpu.HBM),
            pl.BlockSpec(memory_space=pltpu.HBM),
            pl.BlockSpec(memory_space=pltpu.HBM),
            pl.BlockSpec(memory_space=pltpu.HBM),
            pl.BlockSpec(memory_space=pltpu.HBM),
        ],
        out_specs=(pl.BlockSpec(memory_space=pltpu.HBM), pl.BlockSpec(memory_space=pltpu.HBM)),
        scratch_shapes=[
            vmem(mpo.shape[:2] + (2, 2, WB), F32),
            vmem((1, sites), jnp.int32),
            vmem((sites, 3, 2 * DS, DS), BF16),
            vmem((sites, WB * DS, DS), BF16),
            vmem((sites + 1, WB, DS, DS), BF16),
            vmem((sites, WB, DS, DS), BF16),
            vmem((sites, WB, DS, DS), BF16),
            vmem((sites, 2 * DS, DS), BF16),
            vmem((2, WB * DS, WB * DS), BF16),
            vmem((3, 2 * DS, DS), F32),
            vmem((DS, 2 * DS), F32),
            vmem((DS, DS), F32),
            dma((2, sites)),
            dma((sites, 3)),
            dma((sites,)),
            dma((sites, 2)),
            dma((3,)),
            dma((sites, 2)),
            dma((sites, 2)),
            dma((sites, 2)),
            dma((sites, 2)),
        ],
        compiler_params=pltpu.CompilerParams(
            collective_id=0, has_side_effects=True, vmem_limit_bytes=60 * 2**20
        ),
    )(
        jnp.transpose(mpo, (0, 1, 3, 4, 2)),
        jnp.transpose(ranks),
        site_blocks.reshape(states, 2 * DS, DS),
        jnp.transpose(left_carry, (0, 2, 1, 3)),
        sketch.reshape(WB * DS, DS),
    )
    return (
        new_sites.reshape(1, states, DS, 2, DS),
        jnp.transpose(carries, (0, 2, 1, 3))[None],
    )


def solution(mesh):
    return jax.shard_map(
        per_device,
        mesh=mesh,
        in_specs=(
            P("chain", None, "block", None, None),
            P(None, "block", None, None),
            P(),
            P("chain", "block", None, None),
            P(None, "block"),
        ),
        out_specs=(P("chain", None, "block", None, None), P("chain", None, "block", None, None)),
        check_vma=False,
    )
```

```python
import functools

import jax
import jax.numpy as jnp
from jax import lax
from jax.experimental import pallas as pl
from jax.experimental.pallas import tpu as pltpu
from jax.sharding import PartitionSpec as P

CHARGES = (0, 1, -1, 0, 0)
WB = len(CHARGES)
DS = 128
ROWS = 8
EARLY = 3
MESH = pl.DeviceIdType.MESH
F32 = jnp.float32
BF16 = jnp.bfloat16
NN = (((1,), (0,)), ((), ()))
NT = (((1,), (1,)), ((), ()))


def dot(a, b, dims=NN):
    return lax.dot_general(a, b, dims, preferred_element_type=F32)


def halves(x):
    high = x.astype(BF16)
    return high, (x - high.astype(F32)).astype(BF16)


def wide(v, width):
    return v if width == v.shape[1] else jnp.concatenate([v] * (width // v.shape[1]), axis=1)


def invert_factor(work, inverse):
    width = work.shape[1]
    count = DS // ROWS
    part = [slice(i * ROWS, (i + 1) * ROWS) for i in range(count)]

    def lanes(x, first):
        return [jnp.broadcast_to(x[:, first + q : first + q + 1], (ROWS, DS)) for q in range(ROWS)]

    def entry(columns, r, q):
        return jnp.broadcast_to(columns[q][r : r + 1, :], (ROWS, DS))

    rows = work[part[0], :]
    corner = lanes(rows, 0)
    for block in range(count):
        first = block * ROWS
        low = [[entry(corner, r, q) if r >= q else None for q in range(ROWS)] for r in range(ROWS)]
        scale = []
        for q in range(0, ROWS, 2):
            e = q + 1
            inv = lax.rsqrt(low[q][q])
            det = low[q][q] * low[e][e] - low[e][q] * low[e][q]
            inv_e = lax.rsqrt(det) * (low[q][q] * inv)
            scale += [inv, inv_e]
            for r in range(e, ROWS):
                low[r][q] = low[r][q] * inv
            for r in range(e + 1, ROWS):
                low[r][e] = (low[r][e] - low[r][q] * low[e][q]) * inv_e
            for n in range(e + 1, ROWS):
                for r in range(n, ROWS):
                    low[r][n] = low[r][n] - (low[r][q] * low[n][q] + low[r][e] * low[n][e])
        upper = []
        for q in range(ROWS):
            x = jnp.broadcast_to(rows[q : q + 1, :], (ROWS, width))
            for n in range(q):
                x = x - wide(low[q][n], width) * upper[n]
            upper.append(x * wide(scale[q], width))
        for q in range(ROWS):
            inverse[first + q : first + q + 1, :] = upper[q][0:1, DS:]
        if block + 1 == count:
            break
        below = work[part[block + 1], :]
        left = []
        for q, x in enumerate(lanes(below, first)):
            for n in range(q):
                x = x - left[n] * low[q][n]
            left.append(x * scale[q])
        corner = lanes(below, first + ROWS)
        for q in range(ROWS):
            for n in range(ROWS):
                corner[q] = corner[q] - left[n] * jnp.broadcast_to(left[n][q : q + 1, :], (ROWS, DS))
        rows = below
        for q in range(ROWS):
            rows = rows - wide(left[q], width) * upper[q]
        solved = [None] * ROWS
        for q in reversed(range(ROWS)):
            x = upper[q]
            for n in range(q + 1, ROWS):
                x = x - wide(low[n][q], width) * solved[n]
            solved[q] = x * wide(scale[q], width)
        for i in range(block + 2, count):
            rest = work[part[i], :]
            columns = lanes(rest, first)
            for q in range(ROWS):
                rest = rest - wide(columns[q], width) * solved[q]
            work[part[i], :] = rest


def kernel(
    sites, sectors,
    mpo_in, ranks_in, blocks_in, carry_in, sketch_in,
    sites_out, carry_out,
    mpo, ranks, blk, sk, car, sent, below, iso, coupled, plain, work, inverse, base, early, frames, made,
    share_sem, blk_sem, sk_sem, pass_sem, load_sem, t_send, t_recv, o_send, o_recv, e_send, e_recv, m_sem,
):
    c = lax.axis_index("chain")
    p = lax.axis_index("block")
    up = {"block": lax.rem(p + 1, sectors)}
    down = {"block": lax.rem(p + sectors - 1, sectors)}

    def remote(src, dst, send, recv, to):
        return pltpu.make_async_remote_copy(
            src_ref=src, dst_ref=dst, send_sem=send, recv_sem=recv, device_id=to, device_id_type=MESH
        )

    loads = (
        pltpu.make_async_copy(mpo_in, mpo, load_sem.at[0]),
        pltpu.make_async_copy(ranks_in, ranks, load_sem.at[1]),
        pltpu.make_async_copy(carry_in.at[c], car.at[0], load_sem.at[2]),
    )
    pltpu.make_async_copy(blocks_in.at[c], blk.at[c, 0], blk_sem.at[c, 0]).start()
    pltpu.make_async_copy(sketch_in, sk.at[c], sk_sem.at[c]).start()
    for load in loads:
        load.start()

    barrier = pltpu.get_barrier_semaphore()
    for d in range(1, sites):
        pl.semaphore_signal(barrier, inc=1, device_id={"chain": lax.rem(c + d, sites)}, device_id_type=MESH)
    pl.semaphore_signal(barrier, inc=1, device_id=up, device_id_type=MESH)
    pl.semaphore_signal(barrier, inc=1, device_id=down, device_id_type=MESH)
    last = sites - 1

    @pl.when(c == last)
    def _():
        for a in range(last):
            to = {"chain": a, "block": down["block"]}
            pl.semaphore_signal(barrier, inc=1, device_id=to, device_id_type=MESH)

    @pl.when(c == last)
    def _():
        pl.semaphore_wait(barrier, sites + 1)

    @pl.when(c != last)
    def _():
        pl.semaphore_wait(barrier, sites + 2)

    def share(d, which):
        peer = lax.rem(c + d, sites)
        to = {"chain": peer}
        if which == 0:
            return remote(blocks_in.at[peer], blk.at[c, 0], share_sem.at[0, d], blk_sem.at[c, 0], to)
        return remote(sketch_in, sk.at[c], share_sem.at[1, d], sk_sem.at[c], to)

    def passed(k, which, src):
        to = up if which == 0 else down
        return remote(src, blk.at[k, which + 1], pass_sem.at[k, which], blk_sem.at[k, which + 1], to)

    ORDER = (1, sites - 1) + tuple(range(2, sites - 1))

    def share_blocks():
        for d in ORDER:
            share(d, 0).start()
        for which in range(2):
            passed(c, which, blocks_in.at[c]).start()

    def share_sketch():
        for d in ORDER:
            share(d, 1).start()

    def arrived(ref, sem):
        pltpu.make_async_copy(ref, ref, sem).wait()

    def pass_on(k):
        arrived(blk.at[k, 0], blk_sem.at[k, 0])

        @pl.when(c != k)
        def _():
            for which in range(2):
                passed(k, which, blk.at[k, 0]).start()

    top = (p < sectors - 1).astype(F32)
    below_top = (p < sectors - 2).astype(F32)
    bottom = (p > 0).astype(F32)

    def prepare(k):
        for w in range(WB):
            where = {0: 0, 1: 1, -1: 2}[CHARGES[w]]
            if w < 3:
                if where:
                    arrived(blk.at[k, where], blk_sem.at[k, where])
                plain[w] = blk[k, where].astype(F32)
            own = [plain[where, pl.ds(s, DS, stride=2), :] for s in range(2)]
            for v in range(WB):
                for t in range(2):
                    s = t - CHARGES[v] + CHARGES[w]
                    if s not in (0, 1):
                        continue
                    weight = mpo[k, w, t, s : s + 1, v : v + 1]
                    if where == 0 and s == 1:
                        weight = weight * top
                    elif where == 1:
                        weight = weight * bottom
                    elif where == 2:
                        weight = weight * (top if s == 0 else below_top)
                    coupled[t, pl.ds(w * DS, DS), pl.ds(v * DS, DS)] = (own[s] * weight).astype(BF16)

    share_blocks()
    share_sketch()

    for t in range(2):
        for w in range(WB):
            for v in range(WB):
                if t - CHARGES[v] + CHARGES[w] not in (0, 1):
                    coupled[t, pl.ds(w * DS, DS), pl.ds(v * DS, DS)] = jnp.zeros((DS, DS), BF16)
    for load in loads:
        load.wait()
    pass_on(0)
    prepare(0)

    rest = pl.ds(EARLY, WB - EARLY)

    def outgoing(k, which):
        if which == 0:
            ends = iso.at[k], sites_out.at[c]
        else:
            ends = car.at[k + 1], carry_out.at[c]
        return remote(*ends, o_send.at[k, which], o_recv.at[c, which], {"chain": k})

    def final(which, peer):
        if which == 0:
            ends = iso.at[last], frames.at[peer]
        else:
            ends = car.at[sites, rest], carry_out.at[peer, rest]
        return remote(*ends, o_send.at[last, which], o_recv.at[peer, which], {"chain": last})

    def kept(k, which):
        if which == 0:
            return pltpu.make_async_copy(iso.at[k], sites_out.at[c], o_send.at[k, 0])
        return pltpu.make_async_copy(car.at[k + 1], carry_out.at[c], o_send.at[k, 1])

    def ahead(which, peer):
        cut = pl.ds(0, EARLY)
        if which == 0:
            src, to = base, {"chain": last}
        else:
            src, to = sent.at[last, cut], {"chain": last, "block": up["block"]}
        return remote(src, early.at[peer, which], e_send.at[which], e_recv.at[peer, which], to)

    def deliver(k, which):
        @pl.when(c == k)
        def _():
            kept(k, which).start()

        @pl.when(jnp.logical_and(c != k, k < last))
        def _():
            outgoing(k, which).start()

        @pl.when(jnp.logical_and(c != k, k == last))
        def _():
            final(which, c).start()

    row_ids = lax.broadcasted_iota(jnp.int32, (DS, DS), 0)
    column_ids = lax.broadcasted_iota(jnp.int32, (DS, DS), 1)
    rows_f = row_ids.astype(F32)
    site_ids = lax.broadcasted_iota(jnp.int32, (1, sites), 1)
    CUTS = ((0, 3), (3, WB))

    def raised(k, part):
        v0, v1 = CUTS[part]
        cut = pl.ds(v0, v1 - v0)
        return remote(sent.at[k, cut], below.at[k, cut], t_send.at[k, part], t_recv.at[k, part], up)

    def step(k, carry):
        carried = jnp.concatenate([car[k, w] for w in range(WB)], axis=1)
        for part, (v0, v1) in enumerate(CUTS):
            rows = dot(carried, coupled[1, :, pl.ds(v0 * DS, (v1 - v0) * DS)]).astype(BF16)
            for v in range(v0, v1):
                sent[k, v] = rows[:, (v - v0) * DS : (v - v0 + 1) * DS]
            raised(k, part).start()
        hand_on = jnp.logical_and(k == last, c != last)

        @pl.when(hand_on)
        def _():
            ahead(1, c).start()

        terms = dot(carried, coupled[0]).astype(BF16)

        @pl.when(hand_on)
        def _():
            for v in range(EARLY):
                base[v] = terms[:, v * DS : (v + 1) * DS]
            ahead(0, c).start()

        arrived(sk.at[k], sk_sem.at[k])
        tests = sk[k].T
        rank = jnp.sum(jnp.where(site_ids == k, ranks[...].astype(F32), 0.0), axis=1, keepdims=True)
        upper_rank = rank * bottom
        y0 = jnp.where(rows_f < rank, dot(tests, terms, NT), 0.0)

        @pl.when(k == 0)
        def _():
            for later in range(1, sites):
                pass_on(later)

        for part in range(len(CUTS)):
            raised(k, part).wait_recv()
        lower = jnp.concatenate([below[k, v] for v in range(WB)], axis=1)
        y1 = jnp.where(rows_f < upper_rank, dot(tests, lower, NT), 0.0)
        y = jnp.concatenate([y0, y1], axis=1).astype(BF16)
        gram = dot(y, y, NT)
        ridge = jnp.where(rows_f < rank, DS / 4.0, 1.0)
        work[:, :DS] = gram + jnp.where(row_ids == column_ids, ridge, 0.0)
        work[:, DS:] = jnp.where(row_ids == column_ids, 1.0, 0.0)
        invert_factor(work, inverse)

        inv_high, inv_low = halves(inverse[...])
        frame = dot(jnp.concatenate([inv_high, inv_low], axis=1), jnp.concatenate([y, y], axis=0))
        plain[0, pl.ds(0, DS, stride=2), :] = frame[:, :DS]
        plain[0, pl.ds(1, DS, stride=2), :] = frame[:, DS:]
        iso[k] = plain[0].astype(BF16)
        deliver(k, 0)
        new = dot(frame.astype(BF16), jnp.concatenate([terms, lower], axis=0)).astype(BF16)
        for v in range(WB):
            car[k + 1, v] = new[:, v * DS : (v + 1) * DS]
        deliver(k, 1)

        @pl.when(k + 1 < sites)
        def _():
            prepare(k + 1)

        return carry

    lax.fori_loop(0, sites, step, 0)

    for d in range(1, sites):
        for which in range(2):
            share(d, which).wait_send()
    for k in range(sites):
        for part in range(2):
            passed(k, part, blk.at[k, 0]).wait_send()
            raised(k, part).wait_send()

        @pl.when(c == k)
        def _():
            for which in range(2):
                kept(k, which).wait()

        @pl.when(c != k)
        def _():
            for which in range(2):
                (outgoing(k, which) if k < last else final(which, c)).wait_send()

    @pl.when(c != last)
    def _():
        for which in range(2):
            ahead(which, c).wait_send()
        for d in range(1, sites):
            peer = lax.rem(c + d, sites)
            to = {"chain": peer}
            remote(iso.at[0], sites_out.at[peer], o_send.at[0, 0], o_recv.at[peer, 0], to).wait_recv()
            remote(car.at[1], carry_out.at[peer], o_send.at[0, 1], o_recv.at[peer, 1], to).wait_recv()

    @pl.when(c == last)
    def _():
        placed = [
            (
                pltpu.make_async_copy(frames.at[a], sites_out.at[a], m_sem.at[a, 0]),
                pltpu.make_async_copy(made.at[a], carry_out.at[a, pl.ds(0, EARLY)], m_sem.at[a, 1]),
            )
            for a in range(last)
        ]
        for a in range(last):
            ahead(0, a).wait_recv()
            ahead(1, a).wait_recv()
            final(0, a).wait_recv()
            placed[a][0].start()
            plain[0] = frames[a].astype(F32)
            frame = jnp.concatenate([plain[0, pl.ds(t, DS, stride=2), :] for t in range(2)], axis=1).astype(BF16)
            rows = jnp.concatenate(
                [jnp.concatenate([early[a, t, v] for v in range(EARLY)], axis=1) for t in range(2)], axis=0
            )
            new = dot(frame, rows).astype(BF16)
            for v in range(EARLY):
                made[a, v] = new[:, v * DS : (v + 1) * DS]
            placed[a][1].start()
        for a in range(last):
            final(1, a).wait_recv()
            for copy in placed[a]:
                copy.wait()


def keep(sites_in, carry_in, sites_out, carry_out, sem):
    copies = (
        pltpu.make_async_copy(carry_in, carry_out, sem.at[0]),
        pltpu.make_async_copy(sites_in, sites_out, sem.at[1]),
    )
    for copy in copies:
        copy.start()
    for copy in copies:
        copy.wait()


def per_device(site_blocks, left_carry, mpo, sketch, ranks):
    sites = lax.axis_size("chain")
    sectors = lax.axis_size("block")
    states = left_carry.shape[0]
    dma = pltpu.SemaphoreType.DMA
    vmem = pltpu.VMEM
    new_sites, carries = pl.pallas_call(
        functools.partial(kernel, sites, sectors),
        name="zip_up",
        out_shape=(
            jax.ShapeDtypeStruct((states, 2 * DS, DS), BF16),
            jax.ShapeDtypeStruct((states, WB, DS, DS), BF16),
        ),
        in_specs=[
            pl.BlockSpec(memory_space=pltpu.HBM),
            pl.BlockSpec(memory_space=pltpu.HBM),
            pl.BlockSpec(memory_space=pltpu.HBM),
            pl.BlockSpec(memory_space=pltpu.HBM),
            pl.BlockSpec(memory_space=pltpu.HBM),
        ],
        out_specs=(pl.BlockSpec(memory_space=pl.ANY), pl.BlockSpec(memory_space=pl.ANY)),
        scratch_shapes=[
            vmem(mpo.shape[:2] + (2, 2, WB), F32),
            vmem((1, sites), jnp.int32),
            vmem((sites, 3, 2 * DS, DS), BF16),
            vmem((sites, WB * DS, DS), BF16),
            vmem((sites + 1, WB, DS, DS), BF16),
            vmem((sites, WB, DS, DS), BF16),
            vmem((sites, WB, DS, DS), BF16),
            vmem((sites, 2 * DS, DS), BF16),
            vmem((2, WB * DS, WB * DS), BF16),
            vmem((3, 2 * DS, DS), F32),
            vmem((DS, 2 * DS), F32),
            vmem((DS, DS), F32),
            vmem((EARLY, DS, DS), BF16),
            vmem((sites, 2, EARLY, DS, DS), BF16),
            vmem((sites, 2 * DS, DS), BF16),
            vmem((sites, EARLY, DS, DS), BF16),
            dma((2, sites)),
            dma((sites, 3)),
            dma((sites,)),
            dma((sites, 2)),
            dma((3,)),
            dma((sites, 2)),
            dma((sites, 2)),
            dma((sites, 2)),
            dma((sites, 2)),
            dma((2,)),
            dma((sites, 2)),
            dma((sites, 2)),
        ],
        compiler_params=pltpu.CompilerParams(
            collective_id=0, has_side_effects=True, vmem_limit_bytes=40 * 2**20
        ),
    )(*(pltpu.with_memory_space_constraint(x, pltpu.HBM) for x in (
        jnp.transpose(mpo, (0, 1, 3, 4, 2)),
        jnp.transpose(ranks),
        site_blocks.reshape(states, 2 * DS, DS),
        jnp.transpose(left_carry, (0, 2, 1, 3)),
        sketch.reshape(WB * DS, DS),
    )))
    new_sites, carries = pl.pallas_call(
        keep,
        name="keep",
        out_shape=(
            jax.ShapeDtypeStruct(new_sites.shape, BF16),
            jax.ShapeDtypeStruct(carries.shape, BF16),
        ),
        in_specs=[pl.BlockSpec(memory_space=pl.ANY)] * 2,
        out_specs=(pl.BlockSpec(memory_space=pltpu.HBM), pl.BlockSpec(memory_space=pltpu.HBM)),
        scratch_shapes=[dma((2,))],
        compiler_params=pltpu.CompilerParams(vmem_limit_bytes=2**20),
    )(new_sites, carries)
    return (
        new_sites.reshape(1, states, DS, 2, DS),
        jnp.transpose(carries, (0, 2, 1, 3))[None],
    )


def solution(mesh):
    return jax.shard_map(
        per_device,
        mesh=mesh,
        in_specs=(
            P("chain", None, "block", None, None),
            P(None, "block", None, None),
            P(),
            P("chain", "block", None, None),
            P(None, "block"),
        ),
        out_specs=(P("chain", None, "block", None, None), P("chain", None, "block", None, None)),
        check_vma=False,
    )
```

```python
import functools

import jax
import jax.numpy as jnp
from jax import lax
from jax.experimental import pallas as pl
from jax.experimental.pallas import tpu as pltpu
from jax.sharding import PartitionSpec as P

CHARGES = (0, 1, -1, 0, 0)
WB = len(CHARGES)
DS = 128
ROWS = 8
EARLY = 3
MESH = pl.DeviceIdType.MESH
F32 = jnp.float32
BF16 = jnp.bfloat16
NN = (((1,), (0,)), ((), ()))
NT = (((1,), (1,)), ((), ()))


def dot(a, b, dims=NN):
    return lax.dot_general(a, b, dims, preferred_element_type=F32)


def halves(x):
    high = x.astype(BF16)
    return high, (x - high.astype(F32)).astype(BF16)


def wide(v, width):
    return v if width == v.shape[1] else jnp.concatenate([v] * (width // v.shape[1]), axis=1)


def invert_factor(work, inverse):
    width = work.shape[1]
    count = DS // ROWS
    part = [slice(i * ROWS, (i + 1) * ROWS) for i in range(count)]

    def lanes(x, first):
        return [jnp.broadcast_to(x[:, first + q : first + q + 1], (ROWS, DS)) for q in range(ROWS)]

    def entry(columns, r, q):
        return jnp.broadcast_to(columns[q][r : r + 1, :], (ROWS, DS))

    rows = work[part[0], :]
    corner = lanes(rows, 0)
    for block in range(count):
        first = block * ROWS
        low = [[entry(corner, r, q) if r >= q else None for q in range(ROWS)] for r in range(ROWS)]
        scale = []
        for q in range(0, ROWS, 2):
            e = q + 1
            inv = lax.rsqrt(low[q][q])
            det = low[q][q] * low[e][e] - low[e][q] * low[e][q]
            inv_e = lax.rsqrt(det) * (low[q][q] * inv)
            scale += [inv, inv_e]
            for r in range(e, ROWS):
                low[r][q] = low[r][q] * inv
            for r in range(e + 1, ROWS):
                low[r][e] = (low[r][e] - low[r][q] * low[e][q]) * inv_e
            for n in range(e + 1, ROWS):
                for r in range(n, ROWS):
                    low[r][n] = low[r][n] - (low[r][q] * low[n][q] + low[r][e] * low[n][e])
        upper = []
        for q in range(ROWS):
            x = jnp.broadcast_to(rows[q : q + 1, :], (ROWS, width))
            for n in range(q):
                x = x - wide(low[q][n], width) * upper[n]
            upper.append(x * wide(scale[q], width))
        for q in range(ROWS):
            inverse[first + q : first + q + 1, :] = upper[q][0:1, DS:]
        if block + 1 == count:
            break
        below = work[part[block + 1], :]
        left = []
        for q, x in enumerate(lanes(below, first)):
            for n in range(q):
                x = x - left[n] * low[q][n]
            left.append(x * scale[q])
        corner = lanes(below, first + ROWS)
        for q in range(ROWS):
            for n in range(ROWS):
                corner[q] = corner[q] - left[n] * jnp.broadcast_to(left[n][q : q + 1, :], (ROWS, DS))
        rows = below
        for q in range(ROWS):
            rows = rows - wide(left[q], width) * upper[q]
        solved = [None] * ROWS
        for q in reversed(range(ROWS)):
            x = upper[q]
            for n in range(q + 1, ROWS):
                x = x - wide(low[n][q], width) * solved[n]
            solved[q] = x * wide(scale[q], width)
        for i in range(block + 2, count):
            rest = work[part[i], :]
            columns = lanes(rest, first)
            for q in range(ROWS):
                rest = rest - wide(columns[q], width) * solved[q]
            work[part[i], :] = rest


def kernel(
    sites, sectors,
    mpo_in, ranks_in, blocks_in, carry_in, sketch_in,
    sites_out, carry_out,
    mpo, ranks, blk, sk, car, sent, below, iso, coupled, plain, work, inverse, base, early, frames, made,
    share_sem, blk_sem, sk_sem, pass_sem, load_sem, t_send, t_recv, o_send, o_recv, e_send, e_recv, m_sem,
):
    c = lax.axis_index("chain")
    p = lax.axis_index("block")
    up = {"block": lax.rem(p + 1, sectors)}
    down = {"block": lax.rem(p + sectors - 1, sectors)}

    def remote(src, dst, send, recv, to):
        return pltpu.make_async_remote_copy(
            src_ref=src, dst_ref=dst, send_sem=send, recv_sem=recv, device_id=to, device_id_type=MESH
        )

    loads = (
        pltpu.make_async_copy(mpo_in, mpo, load_sem.at[0]),
        pltpu.make_async_copy(ranks_in, ranks, load_sem.at[1]),
        pltpu.make_async_copy(carry_in.at[c], car.at[0], load_sem.at[2]),
    )
    pltpu.make_async_copy(blocks_in.at[c], blk.at[c, 0], blk_sem.at[c, 0]).start()
    pltpu.make_async_copy(sketch_in, sk.at[c], sk_sem.at[c]).start()
    for load in loads:
        load.start()

    barrier = pltpu.get_barrier_semaphore()
    for d in range(1, sites):
        pl.semaphore_signal(barrier, inc=1, device_id={"chain": lax.rem(c + d, sites)}, device_id_type=MESH)
    pl.semaphore_signal(barrier, inc=1, device_id=up, device_id_type=MESH)
    pl.semaphore_signal(barrier, inc=1, device_id=down, device_id_type=MESH)
    last = sites - 1

    @pl.when(c == last)
    def _():
        for a in range(last):
            to = {"chain": a, "block": down["block"]}
            pl.semaphore_signal(barrier, inc=1, device_id=to, device_id_type=MESH)

    @pl.when(c == last)
    def _():
        pl.semaphore_wait(barrier, sites + 1)

    @pl.when(c != last)
    def _():
        pl.semaphore_wait(barrier, sites + 2)

    def share(d, which):
        peer = lax.rem(c + d, sites)
        to = {"chain": peer}
        if which == 0:
            return remote(blocks_in.at[peer], blk.at[c, 0], share_sem.at[0, d], blk_sem.at[c, 0], to)
        return remote(sketch_in, sk.at[c], share_sem.at[1, d], sk_sem.at[c], to)

    def passed(k, which, src):
        to = up if which == 0 else down
        return remote(src, blk.at[k, which + 1], pass_sem.at[k, which], blk_sem.at[k, which + 1], to)

    ORDER = (1, sites - 1) + tuple(range(2, sites - 1))

    def share_blocks():
        for d in ORDER:
            share(d, 0).start()
        for which in range(2):
            passed(c, which, blocks_in.at[c]).start()

    def share_sketch():
        for d in ORDER:
            share(d, 1).start()

    def arrived(ref, sem):
        pltpu.make_async_copy(ref, ref, sem).wait()

    def pass_on(k):
        arrived(blk.at[k, 0], blk_sem.at[k, 0])

        @pl.when(c != k)
        def _():
            for which in range(2):
                passed(k, which, blk.at[k, 0]).start()

    top = (p < sectors - 1).astype(F32)
    below_top = (p < sectors - 2).astype(F32)
    bottom = (p > 0).astype(F32)

    def prepare(k):
        for w in range(WB):
            where = {0: 0, 1: 1, -1: 2}[CHARGES[w]]
            if w < 3:
                if where:
                    arrived(blk.at[k, where], blk_sem.at[k, where])
                plain[w] = blk[k, where].astype(F32)
            own = [plain[where, pl.ds(s, DS, stride=2), :] for s in range(2)]
            for v in range(WB):
                for t in range(2):
                    s = t - CHARGES[v] + CHARGES[w]
                    if s not in (0, 1):
                        continue
                    weight = mpo[k, w, t, s : s + 1, v : v + 1]
                    if where == 0 and s == 1:
                        weight = weight * top
                    elif where == 1:
                        weight = weight * bottom
                    elif where == 2:
                        weight = weight * (top if s == 0 else below_top)
                    coupled[lax.rem(k, 2), t, pl.ds(w * DS, DS), pl.ds(v * DS, DS)] = (own[s] * weight).astype(BF16)

    share_blocks()
    share_sketch()

    for t in range(2):
        for w in range(WB):
            for v in range(WB):
                if t - CHARGES[v] + CHARGES[w] not in (0, 1):
                    for turn in range(2):
                        coupled[turn, t, pl.ds(w * DS, DS), pl.ds(v * DS, DS)] = jnp.zeros((DS, DS), BF16)
    for load in loads:
        load.wait()
    pass_on(0)
    prepare(0)

    rest = pl.ds(EARLY, WB - EARLY)

    def outgoing(k, which):
        if which == 0:
            ends = iso.at[k], sites_out.at[c]
        else:
            ends = car.at[k + 1], carry_out.at[c]
        return remote(*ends, o_send.at[k, which], o_recv.at[c, which], {"chain": k})

    def final(which, peer):
        if which == 0:
            ends = iso.at[last], frames.at[peer]
        else:
            ends = car.at[sites, rest], carry_out.at[peer, rest]
        return remote(*ends, o_send.at[last, which], o_recv.at[peer, which], {"chain": last})

    def kept(k, which):
        if which == 0:
            return pltpu.make_async_copy(iso.at[k], sites_out.at[c], o_send.at[k, 0])
        return pltpu.make_async_copy(car.at[k + 1], carry_out.at[c], o_send.at[k, 1])

    def ahead(which, peer):
        cut = pl.ds(0, EARLY)
        if which == 0:
            src, to = base, {"chain": last}
        else:
            src, to = sent.at[last, cut], {"chain": last, "block": up["block"]}
        return remote(src, early.at[peer, which], e_send.at[which], e_recv.at[peer, which], to)

    def deliver(k, which):
        @pl.when(c == k)
        def _():
            kept(k, which).start()

        @pl.when(jnp.logical_and(c != k, k < last))
        def _():
            outgoing(k, which).start()

        @pl.when(jnp.logical_and(c != k, k == last))
        def _():
            final(which, c).start()

    row_ids = lax.broadcasted_iota(jnp.int32, (DS, DS), 0)
    column_ids = lax.broadcasted_iota(jnp.int32, (DS, DS), 1)
    rows_f = row_ids.astype(F32)
    site_ids = lax.broadcasted_iota(jnp.int32, (1, sites), 1)
    CUTS = ((0, 3), (3, WB))

    def raised(k, part):
        v0, v1 = CUTS[part]
        cut = pl.ds(v0, v1 - v0)
        return remote(sent.at[k, cut], below.at[k, cut], t_send.at[k, part], t_recv.at[k, part], up)

    def step(k, carry):
        carried = jnp.concatenate([car[k, w] for w in range(WB)], axis=1)
        for part, (v0, v1) in enumerate(CUTS):
            rows = dot(carried, coupled[lax.rem(k, 2), 1, :, pl.ds(v0 * DS, (v1 - v0) * DS)]).astype(BF16)
            for v in range(v0, v1):
                sent[k, v] = rows[:, (v - v0) * DS : (v - v0 + 1) * DS]
            raised(k, part).start()
        hand_on = jnp.logical_and(k == last, c != last)

        @pl.when(hand_on)
        def _():
            ahead(1, c).start()

        terms = dot(carried, coupled[lax.rem(k, 2), 0]).astype(BF16)

        @pl.when(hand_on)
        def _():
            for v in range(EARLY):
                base[v] = terms[:, v * DS : (v + 1) * DS]
            ahead(0, c).start()

        arrived(sk.at[k], sk_sem.at[k])
        tests = sk[k].T
        rank = jnp.sum(jnp.where(site_ids == k, ranks[...].astype(F32), 0.0), axis=1, keepdims=True)
        upper_rank = rank * bottom
        y0 = jnp.where(rows_f < rank, dot(tests, terms, NT), 0.0)

        @pl.when(k == 0)
        def _():
            for later in range(1, sites):
                pass_on(later)

        @pl.when(jnp.logical_and(k > 0, k + 1 < sites))
        def _():
            prepare(k + 1)

        for part in range(len(CUTS)):
            raised(k, part).wait_recv()
        lower = jnp.concatenate([below[k, v] for v in range(WB)], axis=1)
        y1 = jnp.where(rows_f < upper_rank, dot(tests, lower, NT), 0.0)
        y = jnp.concatenate([y0, y1], axis=1).astype(BF16)
        gram = dot(y, y, NT)
        ridge = jnp.where(rows_f < rank, DS / 4.0, 1.0)
        work[:, :DS] = gram + jnp.where(row_ids == column_ids, ridge, 0.0)
        work[:, DS:] = jnp.where(row_ids == column_ids, 1.0, 0.0)
        invert_factor(work, inverse)

        inv_high, inv_low = halves(inverse[...])
        frame = dot(jnp.concatenate([inv_high, inv_low], axis=1), jnp.concatenate([y, y], axis=0))
        plain[0, pl.ds(0, DS, stride=2), :] = frame[:, :DS]
        plain[0, pl.ds(1, DS, stride=2), :] = frame[:, DS:]
        iso[k] = plain[0].astype(BF16)
        deliver(k, 0)
        new = dot(frame.astype(BF16), jnp.concatenate([terms, lower], axis=0)).astype(BF16)
        for v in range(WB):
            car[k + 1, v] = new[:, v * DS : (v + 1) * DS]
        deliver(k, 1)

        @pl.when(k == 0)
        def _():
            prepare(1)

        return carry

    lax.fori_loop(0, sites, step, 0)

    for d in range(1, sites):
        for which in range(2):
            share(d, which).wait_send()
    for k in range(sites):
        for part in range(2):
            passed(k, part, blk.at[k, 0]).wait_send()
            raised(k, part).wait_send()

        @pl.when(c == k)
        def _():
            for which in range(2):
                kept(k, which).wait()

        @pl.when(c != k)
        def _():
            for which in range(2):
                (outgoing(k, which) if k < last else final(which, c)).wait_send()

    @pl.when(c != last)
    def _():
        for which in range(2):
            ahead(which, c).wait_send()
        for d in range(1, sites):
            peer = lax.rem(c + d, sites)
            to = {"chain": peer}
            remote(iso.at[0], sites_out.at[peer], o_send.at[0, 0], o_recv.at[peer, 0], to).wait_recv()
            remote(car.at[1], carry_out.at[peer], o_send.at[0, 1], o_recv.at[peer, 1], to).wait_recv()

    @pl.when(c == last)
    def _():
        placed = [
            (
                pltpu.make_async_copy(frames.at[a], sites_out.at[a], m_sem.at[a, 0]),
                pltpu.make_async_copy(made.at[a], carry_out.at[a, pl.ds(0, EARLY)], m_sem.at[a, 1]),
            )
            for a in range(last)
        ]
        for a in range(last):
            ahead(0, a).wait_recv()
            ahead(1, a).wait_recv()
            final(0, a).wait_recv()
            placed[a][0].start()
            plain[0] = frames[a].astype(F32)
            frame = jnp.concatenate([plain[0, pl.ds(t, DS, stride=2), :] for t in range(2)], axis=1).astype(BF16)
            rows = jnp.concatenate(
                [jnp.concatenate([early[a, t, v] for v in range(EARLY)], axis=1) for t in range(2)], axis=0
            )
            new = dot(frame, rows).astype(BF16)
            for v in range(EARLY):
                made[a, v] = new[:, v * DS : (v + 1) * DS]
            placed[a][1].start()
        for a in range(last):
            final(1, a).wait_recv()
            for copy in placed[a]:
                copy.wait()


def keep(sites_in, carry_in, sites_out, carry_out, sem):
    copies = (
        pltpu.make_async_copy(carry_in, carry_out, sem.at[0]),
        pltpu.make_async_copy(sites_in, sites_out, sem.at[1]),
    )
    for copy in copies:
        copy.start()
    for copy in copies:
        copy.wait()


def per_device(site_blocks, left_carry, mpo, sketch, ranks):
    sites = lax.axis_size("chain")
    sectors = lax.axis_size("block")
    states = left_carry.shape[0]
    dma = pltpu.SemaphoreType.DMA
    vmem = pltpu.VMEM
    new_sites, carries = pl.pallas_call(
        functools.partial(kernel, sites, sectors),
        name="zip_up",
        out_shape=(
            jax.ShapeDtypeStruct((states, 2 * DS, DS), BF16),
            jax.ShapeDtypeStruct((states, WB, DS, DS), BF16),
        ),
        in_specs=[
            pl.BlockSpec(memory_space=pltpu.HBM),
            pl.BlockSpec(memory_space=pltpu.HBM),
            pl.BlockSpec(memory_space=pltpu.HBM),
            pl.BlockSpec(memory_space=pltpu.HBM),
            pl.BlockSpec(memory_space=pltpu.HBM),
        ],
        out_specs=(pl.BlockSpec(memory_space=pl.ANY), pl.BlockSpec(memory_space=pl.ANY)),
        scratch_shapes=[
            vmem(mpo.shape[:2] + (2, 2, WB), F32),
            vmem((1, sites), jnp.int32),
            vmem((sites, 3, 2 * DS, DS), BF16),
            vmem((sites, WB * DS, DS), BF16),
            vmem((sites + 1, WB, DS, DS), BF16),
            vmem((sites, WB, DS, DS), BF16),
            vmem((sites, WB, DS, DS), BF16),
            vmem((sites, 2 * DS, DS), BF16),
            vmem((2, 2, WB * DS, WB * DS), BF16),
            vmem((3, 2 * DS, DS), F32),
            vmem((DS, 2 * DS), F32),
            vmem((DS, DS), F32),
            vmem((EARLY, DS, DS), BF16),
            vmem((sites, 2, EARLY, DS, DS), BF16),
            vmem((sites, 2 * DS, DS), BF16),
            vmem((sites, EARLY, DS, DS), BF16),
            dma((2, sites)),
            dma((sites, 3)),
            dma((sites,)),
            dma((sites, 2)),
            dma((3,)),
            dma((sites, 2)),
            dma((sites, 2)),
            dma((sites, 2)),
            dma((sites, 2)),
            dma((2,)),
            dma((sites, 2)),
            dma((sites, 2)),
        ],
        compiler_params=pltpu.CompilerParams(
            collective_id=0, has_side_effects=True, vmem_limit_bytes=40 * 2**20
        ),
    )(*(pltpu.with_memory_space_constraint(x, pltpu.HBM) for x in (
        jnp.transpose(mpo, (0, 1, 3, 4, 2)),
        jnp.transpose(ranks),
        site_blocks.reshape(states, 2 * DS, DS),
        jnp.transpose(left_carry, (0, 2, 1, 3)),
        sketch.reshape(WB * DS, DS),
    )))
    new_sites, carries = pl.pallas_call(
        keep,
        name="keep",
        out_shape=(
            jax.ShapeDtypeStruct(new_sites.shape, BF16),
            jax.ShapeDtypeStruct(carries.shape, BF16),
        ),
        in_specs=[pl.BlockSpec(memory_space=pl.ANY)] * 2,
        out_specs=(pl.BlockSpec(memory_space=pltpu.HBM), pl.BlockSpec(memory_space=pltpu.HBM)),
        scratch_shapes=[dma((2,))],
        compiler_params=pltpu.CompilerParams(vmem_limit_bytes=2**20),
    )(new_sites, carries)
    return (
        new_sites.reshape(1, states, DS, 2, DS),
        jnp.transpose(carries, (0, 2, 1, 3))[None],
    )


def solution(mesh):
    return jax.shard_map(
        per_device,
        mesh=mesh,
        in_specs=(
            P("chain", None, "block", None, None),
            P(None, "block", None, None),
            P(),
            P("chain", "block", None, None),
            P(None, "block"),
        ),
        out_specs=(P("chain", None, "block", None, None), P("chain", None, "block", None, None)),
        check_vma=False,
    )
```

```python
import functools

import jax
import jax.numpy as jnp
from jax import lax
from jax.experimental import pallas as pl
from jax.experimental.pallas import tpu as pltpu
from jax.sharding import PartitionSpec as P

CHARGES = (0, 1, -1, 0, 0)
WB = len(CHARGES)
DS = 128
ROWS = 8
EARLY = 3
MESH = pl.DeviceIdType.MESH
F32 = jnp.float32
BF16 = jnp.bfloat16
NN = (((1,), (0,)), ((), ()))
NT = (((1,), (1,)), ((), ()))


def dot(a, b, dims=NN):
    return lax.dot_general(a, b, dims, preferred_element_type=F32)


def halves(x):
    high = x.astype(BF16)
    return high, (x - high.astype(F32)).astype(BF16)


def wide(v, width):
    return v if width == v.shape[1] else jnp.concatenate([v] * (width // v.shape[1]), axis=1)


def invert_factor(work, inverse):
    width = work.shape[1]
    count = DS // ROWS
    part = [slice(i * ROWS, (i + 1) * ROWS) for i in range(count)]

    def lanes(x, first):
        return [jnp.broadcast_to(x[:, first + q : first + q + 1], (ROWS, DS)) for q in range(ROWS)]

    def entry(columns, r, q):
        return jnp.broadcast_to(columns[q][r : r + 1, :], (ROWS, DS))

    rows = work[part[0], :]
    corner = lanes(rows, 0)
    for block in range(count):
        first = block * ROWS
        low = [[entry(corner, r, q) if r >= q else None for q in range(ROWS)] for r in range(ROWS)]
        scale = []
        for q in range(0, ROWS, 2):
            e = q + 1
            inv = lax.rsqrt(low[q][q])
            det = low[q][q] * low[e][e] - low[e][q] * low[e][q]
            inv_e = lax.rsqrt(det) * (low[q][q] * inv)
            scale += [inv, inv_e]
            for r in range(e, ROWS):
                low[r][q] = low[r][q] * inv
            for r in range(e + 1, ROWS):
                low[r][e] = (low[r][e] - low[r][q] * low[e][q]) * inv_e
            for n in range(e + 1, ROWS):
                for r in range(n, ROWS):
                    low[r][n] = low[r][n] - (low[r][q] * low[n][q] + low[r][e] * low[n][e])
        upper = []
        for q in range(ROWS):
            x = jnp.broadcast_to(rows[q : q + 1, :], (ROWS, width))
            for n in range(q):
                x = x - wide(low[q][n], width) * upper[n]
            upper.append(x * wide(scale[q], width))
        for q in range(ROWS):
            inverse[first + q : first + q + 1, :] = upper[q][0:1, DS:]
        if block + 1 == count:
            break
        below = work[part[block + 1], :]
        left = []
        for q, x in enumerate(lanes(below, first)):
            for n in range(q):
                x = x - left[n] * low[q][n]
            left.append(x * scale[q])
        corner = lanes(below, first + ROWS)
        for q in range(ROWS):
            for n in range(ROWS):
                corner[q] = corner[q] - left[n] * jnp.broadcast_to(left[n][q : q + 1, :], (ROWS, DS))
        rows = below
        for q in range(ROWS):
            rows = rows - wide(left[q], width) * upper[q]
        solved = [None] * ROWS
        for q in reversed(range(ROWS)):
            x = upper[q]
            for n in range(q + 1, ROWS):
                x = x - wide(low[n][q], width) * solved[n]
            solved[q] = x * wide(scale[q], width)
        for i in range(block + 2, count):
            rest = work[part[i], :]
            columns = lanes(rest, first)
            for q in range(ROWS):
                rest = rest - wide(columns[q], width) * solved[q]
            work[part[i], :] = rest


def kernel(
    sites, sectors,
    mpo_in, ranks_in, blocks_in, carry_in, sketch_in,
    sites_out, carry_out,
    mpo, ranks, blk, sk, car, sent, below, iso, coupled, plain, work, inverse, base, early, frames, made,
    share_sem, blk_sem, sk_sem, pass_sem, load_sem, t_send, t_recv, o_send, o_recv, e_send, e_recv, m_sem,
):
    c = lax.axis_index("chain")
    p = lax.axis_index("block")
    up = {"block": lax.rem(p + 1, sectors)}
    down = {"block": lax.rem(p + sectors - 1, sectors)}

    def remote(src, dst, send, recv, to):
        return pltpu.make_async_remote_copy(
            src_ref=src, dst_ref=dst, send_sem=send, recv_sem=recv, device_id=to, device_id_type=MESH
        )

    loads = (
        pltpu.make_async_copy(mpo_in, mpo, load_sem.at[0]),
        pltpu.make_async_copy(ranks_in, ranks, load_sem.at[1]),
        pltpu.make_async_copy(carry_in.at[c], car.at[0], load_sem.at[2]),
    )
    pltpu.make_async_copy(blocks_in.at[c], blk.at[c, 0], blk_sem.at[c, 0]).start()
    pltpu.make_async_copy(sketch_in, sk.at[c], sk_sem.at[c]).start()
    for load in loads:
        load.start()

    barrier = pltpu.get_barrier_semaphore()
    for d in range(1, sites):
        pl.semaphore_signal(barrier, inc=1, device_id={"chain": lax.rem(c + d, sites)}, device_id_type=MESH)
    pl.semaphore_signal(barrier, inc=1, device_id=up, device_id_type=MESH)
    pl.semaphore_signal(barrier, inc=1, device_id=down, device_id_type=MESH)
    last = sites - 1

    @pl.when(c == last)
    def _():
        for a in range(last):
            to = {"chain": a, "block": down["block"]}
            pl.semaphore_signal(barrier, inc=1, device_id=to, device_id_type=MESH)

    @pl.when(c == last)
    def _():
        pl.semaphore_wait(barrier, sites + 1)

    @pl.when(c != last)
    def _():
        pl.semaphore_wait(barrier, sites + 2)

    def share(d, which):
        peer = lax.rem(c + d, sites)
        to = {"chain": peer}
        if which == 0:
            return remote(blocks_in.at[peer], blk.at[c, 0], share_sem.at[0, d], blk_sem.at[c, 0], to)
        return remote(sketch_in, sk.at[c], share_sem.at[1, d], sk_sem.at[c], to)

    def passed(k, which, src):
        to = up if which == 0 else down
        return remote(src, blk.at[k, which + 1], pass_sem.at[k, which], blk_sem.at[k, which + 1], to)

    ORDER = (1, sites - 1) + tuple(range(2, sites - 1))

    def share_blocks():
        for d in ORDER:
            share(d, 0).start()
        for which in range(2):
            passed(c, which, blocks_in.at[c]).start()

    def share_sketch():
        for d in ORDER:
            share(d, 1).start()

    def arrived(ref, sem):
        pltpu.make_async_copy(ref, ref, sem).wait()

    def pass_on(k):
        arrived(blk.at[k, 0], blk_sem.at[k, 0])

        @pl.when(c != k)
        def _():
            for which in range(2):
                passed(k, which, blk.at[k, 0]).start()

    top = (p < sectors - 1).astype(F32)
    below_top = (p < sectors - 2).astype(F32)
    bottom = (p > 0).astype(F32)

    def prepare(k):
        for w in range(WB):
            where = {0: 0, 1: 1, -1: 2}[CHARGES[w]]
            if w < 3:
                if where:
                    arrived(blk.at[k, where], blk_sem.at[k, where])
                plain[w] = blk[k, where].astype(F32)
            own = [plain[where, pl.ds(s, DS, stride=2), :] for s in range(2)]
            for v in range(WB):
                for t in range(2):
                    s = t - CHARGES[v] + CHARGES[w]
                    if s not in (0, 1):
                        continue
                    weight = mpo[k, w, t, s : s + 1, v : v + 1]
                    if where == 0 and s == 1:
                        weight = weight * top
                    elif where == 1:
                        weight = weight * bottom
                    elif where == 2:
                        weight = weight * (top if s == 0 else below_top)
                    coupled[lax.rem(k, 2), t, pl.ds(w * DS, DS), pl.ds(v * DS, DS)] = (own[s] * weight).astype(BF16)

    share_blocks()
    share_sketch()

    for t in range(2):
        for w in range(WB):
            for v in range(WB):
                if t - CHARGES[v] + CHARGES[w] not in (0, 1):
                    for turn in range(2):
                        coupled[turn, t, pl.ds(w * DS, DS), pl.ds(v * DS, DS)] = jnp.zeros((DS, DS), BF16)
    for load in loads:
        load.wait()
    pass_on(0)
    prepare(0)

    rest = pl.ds(EARLY, WB - EARLY)

    def outgoing(k, which):
        if which == 0:
            ends = iso.at[k], sites_out.at[c]
        else:
            ends = car.at[k + 1], carry_out.at[c]
        return remote(*ends, o_send.at[k, which], o_recv.at[c, which], {"chain": k})

    def final(which, peer):
        if which == 0:
            ends = iso.at[last], frames.at[peer]
        else:
            ends = car.at[sites, rest], carry_out.at[peer, rest]
        return remote(*ends, o_send.at[last, which], o_recv.at[peer, which], {"chain": last})

    def kept(k, which):
        if which == 0:
            return pltpu.make_async_copy(iso.at[k], sites_out.at[c], o_send.at[k, 0])
        return pltpu.make_async_copy(car.at[k + 1], carry_out.at[c], o_send.at[k, 1])

    def ahead(which, peer):
        cut = pl.ds(0, EARLY)
        if which == 0:
            src, to = base, {"chain": last}
        else:
            src, to = sent.at[last, cut], {"chain": last, "block": up["block"]}
        return remote(src, early.at[peer, which], e_send.at[which], e_recv.at[peer, which], to)

    def deliver(k, which):
        @pl.when(c == k)
        def _():
            kept(k, which).start()

        @pl.when(jnp.logical_and(c != k, k < last))
        def _():
            outgoing(k, which).start()

        @pl.when(jnp.logical_and(c != k, k == last))
        def _():
            final(which, c).start()

    row_ids = lax.broadcasted_iota(jnp.int32, (DS, DS), 0)
    column_ids = lax.broadcasted_iota(jnp.int32, (DS, DS), 1)
    rows_f = row_ids.astype(F32)
    site_ids = lax.broadcasted_iota(jnp.int32, (1, sites), 1)
    CUTS = ((0, 3), (3, WB))

    def raised(k, part):
        v0, v1 = CUTS[part]
        cut = pl.ds(v0, v1 - v0)
        return remote(sent.at[k, cut], below.at[k, cut], t_send.at[k, part], t_recv.at[k, part], up)

    def step(k, carry):
        carried = jnp.concatenate([car[k, w] for w in range(WB)], axis=1)
        for part, (v0, v1) in enumerate(CUTS):
            rows = dot(carried, coupled[lax.rem(k, 2), 1, :, pl.ds(v0 * DS, (v1 - v0) * DS)]).astype(BF16)
            for v in range(v0, v1):
                sent[k, v] = rows[:, (v - v0) * DS : (v - v0 + 1) * DS]
            raised(k, part).start()
        hand_on = jnp.logical_and(k == last, c != last)

        @pl.when(hand_on)
        def _():
            ahead(1, c).start()

        terms = dot(carried, coupled[lax.rem(k, 2), 0]).astype(BF16)

        @pl.when(hand_on)
        def _():
            for v in range(EARLY):
                base[v] = terms[:, v * DS : (v + 1) * DS]
            ahead(0, c).start()

        arrived(sk.at[k], sk_sem.at[k])
        tests = sk[k].T
        rank = jnp.sum(jnp.where(site_ids == k, ranks[...].astype(F32), 0.0), axis=1, keepdims=True)
        upper_rank = rank * bottom
        y0 = jnp.where(rows_f < rank, dot(tests, terms, NT), 0.0)

        @pl.when(k == 0)
        def _():
            for later in range(1, sites):
                pass_on(later)

        work[:, DS:] = jnp.where(row_ids == column_ids, 1.0, 0.0)
        ridge = jnp.where(row_ids == column_ids, jnp.where(rows_f < rank, DS / 4.0, 1.0), 0.0)
        @pl.when(jnp.logical_and(k > 0, k + 1 < sites))
        def _():
            prepare(k + 1)

        y1 = 0.0
        for part, (v0, v1) in enumerate(CUTS):
            raised(k, part).wait_recv()
            rows = jnp.concatenate([below[k, v] for v in range(v0, v1)], axis=1)
            y1 = y1 + dot(tests[:, v0 * DS : v1 * DS], rows, NT)
        y1 = jnp.where(rows_f < upper_rank, y1, 0.0)
        lower = jnp.concatenate([below[k, v] for v in range(WB)], axis=1)
        y = jnp.concatenate([y0, y1], axis=1).astype(BF16)
        gram = dot(y, y, NT)
        work[:, :DS] = gram + ridge
        invert_factor(work, inverse)

        inv_high, inv_low = halves(inverse[...])
        frame = dot(jnp.concatenate([inv_high, inv_low], axis=1), jnp.concatenate([y, y], axis=0))
        plain[0, pl.ds(0, DS, stride=2), :] = frame[:, :DS]
        plain[0, pl.ds(1, DS, stride=2), :] = frame[:, DS:]
        iso[k] = plain[0].astype(BF16)
        deliver(k, 0)
        new = dot(frame.astype(BF16), jnp.concatenate([terms, lower], axis=0)).astype(BF16)
        for v in range(WB):
            car[k + 1, v] = new[:, v * DS : (v + 1) * DS]
        deliver(k, 1)

        @pl.when(k == 0)
        def _():
            prepare(1)

        return carry

    lax.fori_loop(0, sites, step, 0)

    for d in range(1, sites):
        for which in range(2):
            share(d, which).wait_send()
    for k in range(sites):
        for part in range(2):
            passed(k, part, blk.at[k, 0]).wait_send()
            raised(k, part).wait_send()

        @pl.when(c == k)
        def _():
            for which in range(2):
                kept(k, which).wait()

        @pl.when(c != k)
        def _():
            for which in range(2):
                (outgoing(k, which) if k < last else final(which, c)).wait_send()

    @pl.when(c != last)
    def _():
        for which in range(2):
            ahead(which, c).wait_send()
        for d in range(1, sites):
            peer = lax.rem(c + d, sites)
            to = {"chain": peer}
            remote(iso.at[0], sites_out.at[peer], o_send.at[0, 0], o_recv.at[peer, 0], to).wait_recv()
            remote(car.at[1], carry_out.at[peer], o_send.at[0, 1], o_recv.at[peer, 1], to).wait_recv()

    @pl.when(c == last)
    def _():
        placed = [
            (
                pltpu.make_async_copy(frames.at[a], sites_out.at[a], m_sem.at[a, 0]),
                pltpu.make_async_copy(made.at[a], carry_out.at[a, pl.ds(0, EARLY)], m_sem.at[a, 1]),
            )
            for a in range(last)
        ]
        for a in sorted(range(last), key=lambda a: min(last - a, a + 1)):
            ahead(0, a).wait_recv()
            ahead(1, a).wait_recv()
            final(0, a).wait_recv()
            placed[a][0].start()
            plain[0] = frames[a].astype(F32)
            frame = jnp.concatenate([plain[0, pl.ds(t, DS, stride=2), :] for t in range(2)], axis=1).astype(BF16)
            rows = jnp.concatenate(
                [jnp.concatenate([early[a, t, v] for v in range(EARLY)], axis=1) for t in range(2)], axis=0
            )
            new = dot(frame, rows).astype(BF16)
            for v in range(EARLY):
                made[a, v] = new[:, v * DS : (v + 1) * DS]
            placed[a][1].start()
        for a in range(last):
            final(1, a).wait_recv()
            for copy in placed[a]:
                copy.wait()


def keep(sites_in, carry_in, sites_out, carry_out, sem):
    copies = (
        pltpu.make_async_copy(carry_in, carry_out, sem.at[0]),
        pltpu.make_async_copy(sites_in, sites_out, sem.at[1]),
    )
    for copy in copies:
        copy.start()
    for copy in copies:
        copy.wait()


def per_device(site_blocks, left_carry, mpo, sketch, ranks):
    sites = lax.axis_size("chain")
    sectors = lax.axis_size("block")
    states = left_carry.shape[0]
    dma = pltpu.SemaphoreType.DMA
    vmem = pltpu.VMEM
    new_sites, carries = pl.pallas_call(
        functools.partial(kernel, sites, sectors),
        name="zip_up",
        out_shape=(
            jax.ShapeDtypeStruct((states, 2 * DS, DS), BF16),
            jax.ShapeDtypeStruct((states, WB, DS, DS), BF16),
        ),
        in_specs=[
            pl.BlockSpec(memory_space=pltpu.HBM),
            pl.BlockSpec(memory_space=pltpu.HBM),
            pl.BlockSpec(memory_space=pltpu.HBM),
            pl.BlockSpec(memory_space=pltpu.HBM),
            pl.BlockSpec(memory_space=pltpu.HBM),
        ],
        out_specs=(pl.BlockSpec(memory_space=pl.ANY), pl.BlockSpec(memory_space=pl.ANY)),
        scratch_shapes=[
            vmem(mpo.shape[:2] + (2, 2, WB), F32),
            vmem((1, sites), jnp.int32),
            vmem((sites, 3, 2 * DS, DS), BF16),
            vmem((sites, WB * DS, DS), BF16),
            vmem((sites + 1, WB, DS, DS), BF16),
            vmem((sites, WB, DS, DS), BF16),
            vmem((sites, WB, DS, DS), BF16),
            vmem((sites, 2 * DS, DS), BF16),
            vmem((2, 2, WB * DS, WB * DS), BF16),
            vmem((3, 2 * DS, DS), F32),
            vmem((DS, 2 * DS), F32),
            vmem((DS, DS), F32),
            vmem((EARLY, DS, DS), BF16),
            vmem((sites, 2, EARLY, DS, DS), BF16),
            vmem((sites, 2 * DS, DS), BF16),
            vmem((sites, EARLY, DS, DS), BF16),
            dma((2, sites)),
            dma((sites, 3)),
            dma((sites,)),
            dma((sites, 2)),
            dma((3,)),
            dma((sites, 2)),
            dma((sites, 2)),
            dma((sites, 2)),
            dma((sites, 2)),
            dma((2,)),
            dma((sites, 2)),
            dma((sites, 2)),
        ],
        compiler_params=pltpu.CompilerParams(
            collective_id=0, has_side_effects=True, vmem_limit_bytes=40 * 2**20
        ),
    )(*(pltpu.with_memory_space_constraint(x, pltpu.HBM) for x in (
        jnp.transpose(mpo, (0, 1, 3, 4, 2)),
        jnp.transpose(ranks),
        site_blocks.reshape(states, 2 * DS, DS),
        jnp.transpose(left_carry, (0, 2, 1, 3)),
        sketch.reshape(WB * DS, DS),
    )))
    new_sites, carries = pl.pallas_call(
        keep,
        name="keep",
        out_shape=(
            jax.ShapeDtypeStruct(new_sites.shape, BF16),
            jax.ShapeDtypeStruct(carries.shape, BF16),
        ),
        in_specs=[pl.BlockSpec(memory_space=pl.ANY)] * 2,
        out_specs=(pl.BlockSpec(memory_space=pltpu.HBM), pl.BlockSpec(memory_space=pltpu.HBM)),
        scratch_shapes=[dma((2,))],
        compiler_params=pltpu.CompilerParams(vmem_limit_bytes=2**20),
    )(new_sites, carries)
    return (
        new_sites.reshape(1, states, DS, 2, DS),
        jnp.transpose(carries, (0, 2, 1, 3))[None],
    )


def solution(mesh):
    return jax.shard_map(
        per_device,
        mesh=mesh,
        in_specs=(
            P("chain", None, "block", None, None),
            P(None, "block", None, None),
            P(),
            P("chain", "block", None, None),
            P(None, "block"),
        ),
        out_specs=(P("chain", None, "block", None, None), P("chain", None, "block", None, None)),
        check_vma=False,
    )
```

```python
import functools

import jax
import jax.numpy as jnp
from jax import lax
from jax.experimental import pallas as pl
from jax.experimental.pallas import tpu as pltpu
from jax.sharding import PartitionSpec as P

CHARGES = (0, 1, -1, 0, 0)
WB = len(CHARGES)
DS = 128
ROWS = 8
EARLY = 3
MESH = pl.DeviceIdType.MESH
F32 = jnp.float32
BF16 = jnp.bfloat16
NN = (((1,), (0,)), ((), ()))
NT = (((1,), (1,)), ((), ()))


def dot(a, b, dims=NN):
    return lax.dot_general(a, b, dims, preferred_element_type=F32)


def halves(x):
    high = x.astype(BF16)
    return high, (x - high.astype(F32)).astype(BF16)


def wide(v, width):
    return v if width == v.shape[1] else jnp.concatenate([v] * (width // v.shape[1]), axis=1)


def invert_factor(work, inverse):
    width = work.shape[1]
    count = DS // ROWS
    part = [slice(i * ROWS, (i + 1) * ROWS) for i in range(count)]

    def lanes(x, first):
        return [jnp.broadcast_to(x[:, first + q : first + q + 1], (ROWS, DS)) for q in range(ROWS)]

    def entry(columns, r, q):
        return jnp.broadcast_to(columns[q][r : r + 1, :], (ROWS, DS))

    rows = work[part[0], :]
    corner = lanes(rows, 0)
    for block in range(count):
        first = block * ROWS
        low = [[entry(corner, r, q) if r >= q else None for q in range(ROWS)] for r in range(ROWS)]
        scale = []
        for q in range(0, ROWS, 2):
            e = q + 1
            inv = lax.rsqrt(low[q][q])
            det = low[q][q] * low[e][e] - low[e][q] * low[e][q]
            inv_e = lax.rsqrt(det) * (low[q][q] * inv)
            scale += [inv, inv_e]
            for r in range(e, ROWS):
                low[r][q] = low[r][q] * inv
            for r in range(e + 1, ROWS):
                low[r][e] = (low[r][e] - low[r][q] * low[e][q]) * inv_e
            for n in range(e + 1, ROWS):
                for r in range(n, ROWS):
                    low[r][n] = low[r][n] - (low[r][q] * low[n][q] + low[r][e] * low[n][e])
        upper = []
        for q in range(ROWS):
            x = jnp.broadcast_to(rows[q : q + 1, :], (ROWS, width))
            for n in range(q):
                x = x - wide(low[q][n], width) * upper[n]
            upper.append(x * wide(scale[q], width))
        for q in range(ROWS):
            inverse[first + q : first + q + 1, :] = upper[q][0:1, DS:]
        if block + 1 == count:
            break
        below = work[part[block + 1], :]
        left = []
        for q, x in enumerate(lanes(below, first)):
            for n in range(q):
                x = x - left[n] * low[q][n]
            left.append(x * scale[q])
        corner = lanes(below, first + ROWS)
        for q in range(ROWS):
            for n in range(ROWS):
                corner[q] = corner[q] - left[n] * jnp.broadcast_to(left[n][q : q + 1, :], (ROWS, DS))
        rows = below
        for q in range(ROWS):
            rows = rows - wide(left[q], width) * upper[q]
        solved = [None] * ROWS
        for q in reversed(range(ROWS)):
            x = upper[q]
            for n in range(q + 1, ROWS):
                x = x - wide(low[n][q], width) * solved[n]
            solved[q] = x * wide(scale[q], width)
        for i in range(block + 2, count):
            rest = work[part[i], :]
            columns = lanes(rest, first)
            for q in range(ROWS):
                rest = rest - wide(columns[q], width) * solved[q]
            work[part[i], :] = rest


def kernel(
    sites, sectors,
    mpo_in, ranks_in, blocks_in, carry_in, sketch_in,
    sites_out, carry_out,
    mpo, ranks, blk, sk, car, sent, below, iso, coupled, plain, work, inverse, base, early, frames, made,
    share_sem, blk_sem, sk_sem, pass_sem, load_sem, t_send, t_recv, o_send, o_recv, e_send, e_recv, m_sem,
):
    c = lax.axis_index("chain")
    p = lax.axis_index("block")
    up = {"block": lax.rem(p + 1, sectors)}
    down = {"block": lax.rem(p + sectors - 1, sectors)}

    def remote(src, dst, send, recv, to):
        return pltpu.make_async_remote_copy(
            src_ref=src, dst_ref=dst, send_sem=send, recv_sem=recv, device_id=to, device_id_type=MESH
        )

    loads = (
        pltpu.make_async_copy(mpo_in, mpo, load_sem.at[0]),
        pltpu.make_async_copy(ranks_in, ranks, load_sem.at[1]),
        pltpu.make_async_copy(carry_in.at[c], car.at[0], load_sem.at[2]),
    )
    pltpu.make_async_copy(blocks_in.at[c], blk.at[c, 0], blk_sem.at[c, 0]).start()
    pltpu.make_async_copy(sketch_in, sk.at[c], sk_sem.at[c]).start()
    for load in loads:
        load.start()

    barrier = pltpu.get_barrier_semaphore()
    for d in range(1, sites):
        pl.semaphore_signal(barrier, inc=1, device_id={"chain": lax.rem(c + d, sites)}, device_id_type=MESH)
    pl.semaphore_signal(barrier, inc=1, device_id=up, device_id_type=MESH)
    pl.semaphore_signal(barrier, inc=1, device_id=down, device_id_type=MESH)
    last = sites - 1

    @pl.when(c == last)
    def _():
        for a in range(last):
            to = {"chain": a, "block": down["block"]}
            pl.semaphore_signal(barrier, inc=1, device_id=to, device_id_type=MESH)

    @pl.when(c == last)
    def _():
        pl.semaphore_wait(barrier, sites + 1)

    @pl.when(c != last)
    def _():
        pl.semaphore_wait(barrier, sites + 2)

    def share(d, which):
        peer = lax.rem(c + d, sites)
        to = {"chain": peer}
        if which == 0:
            return remote(blocks_in.at[peer], blk.at[c, 0], share_sem.at[0, d], blk_sem.at[c, 0], to)
        return remote(sketch_in, sk.at[c], share_sem.at[1, d], sk_sem.at[c], to)

    def passed(k, which, src):
        to = up if which == 0 else down
        return remote(src, blk.at[k, which + 1], pass_sem.at[k, which], blk_sem.at[k, which + 1], to)

    ORDER = (1, sites - 1) + tuple(range(2, sites - 1))

    def share_blocks():
        for which in range(2):
            passed(c, which, blocks_in.at[c]).start()
        for d in ORDER:
            share(d, 0).start()

    def share_sketch():
        for d in ORDER:
            share(d, 1).start()

    def arrived(ref, sem):
        pltpu.make_async_copy(ref, ref, sem).wait()

    def pass_on(k):
        arrived(blk.at[k, 0], blk_sem.at[k, 0])

        @pl.when(c != k)
        def _():
            for which in range(2):
                passed(k, which, blk.at[k, 0]).start()

    top = (p < sectors - 1).astype(F32)
    below_top = (p < sectors - 2).astype(F32)
    bottom = (p > 0).astype(F32)

    def prepare(k):
        for w in range(WB):
            where = {0: 0, 1: 1, -1: 2}[CHARGES[w]]
            if w < 3:
                if where:
                    arrived(blk.at[k, where], blk_sem.at[k, where])
                plain[w] = blk[k, where].astype(F32)
            own = [plain[where, pl.ds(s, DS, stride=2), :] for s in range(2)]
            for v in range(WB):
                for t in range(2):
                    s = t - CHARGES[v] + CHARGES[w]
                    if s not in (0, 1):
                        continue
                    weight = mpo[k, w, t, s : s + 1, v : v + 1]
                    if where == 0 and s == 1:
                        weight = weight * top
                    elif where == 1:
                        weight = weight * bottom
                    elif where == 2:
                        weight = weight * (top if s == 0 else below_top)
                    coupled[lax.rem(k, 2), t, pl.ds(w * DS, DS), pl.ds(v * DS, DS)] = (own[s] * weight).astype(BF16)

    share_blocks()
    share_sketch()

    for t in range(2):
        for w in range(WB):
            for v in range(WB):
                if t - CHARGES[v] + CHARGES[w] not in (0, 1):
                    for turn in range(2):
                        coupled[turn, t, pl.ds(w * DS, DS), pl.ds(v * DS, DS)] = jnp.zeros((DS, DS), BF16)
    for load in loads:
        load.wait()
    pass_on(0)
    prepare(0)

    rest = pl.ds(EARLY, WB - EARLY)

    def outgoing(k, which):
        if which == 0:
            ends = iso.at[k], sites_out.at[c]
        else:
            ends = car.at[k + 1], carry_out.at[c]
        return remote(*ends, o_send.at[k, which], o_recv.at[c, which], {"chain": k})

    def final(which, peer):
        if which == 0:
            ends = iso.at[last], frames.at[peer]
        else:
            ends = car.at[sites, rest], carry_out.at[peer, rest]
        return remote(*ends, o_send.at[last, which], o_recv.at[peer, which], {"chain": last})

    def kept(k, which):
        if which == 0:
            return pltpu.make_async_copy(iso.at[k], sites_out.at[c], o_send.at[k, 0])
        return pltpu.make_async_copy(car.at[k + 1], carry_out.at[c], o_send.at[k, 1])

    def ahead(which, peer):
        cut = pl.ds(0, EARLY)
        if which == 0:
            src, to = base, {"chain": last}
        else:
            src, to = sent.at[last, cut], {"chain": last, "block": up["block"]}
        return remote(src, early.at[peer, which], e_send.at[which], e_recv.at[peer, which], to)

    def deliver(k, which):
        @pl.when(c == k)
        def _():
            kept(k, which).start()

        @pl.when(jnp.logical_and(c != k, k < last))
        def _():
            outgoing(k, which).start()

        @pl.when(jnp.logical_and(c != k, k == last))
        def _():
            final(which, c).start()

    row_ids = lax.broadcasted_iota(jnp.int32, (DS, DS), 0)
    column_ids = lax.broadcasted_iota(jnp.int32, (DS, DS), 1)
    rows_f = row_ids.astype(F32)
    site_ids = lax.broadcasted_iota(jnp.int32, (1, sites), 1)
    CUTS = ((0, 3), (3, WB))

    def raised(k, part):
        v0, v1 = CUTS[part]
        cut = pl.ds(v0, v1 - v0)
        return remote(sent.at[k, cut], below.at[k, cut], t_send.at[k, part], t_recv.at[k, part], up)

    def step(k, carry):
        carried = jnp.concatenate([car[k, w] for w in range(WB)], axis=1)
        for part, (v0, v1) in enumerate(CUTS):
            rows = dot(carried, coupled[lax.rem(k, 2), 1, :, pl.ds(v0 * DS, (v1 - v0) * DS)]).astype(BF16)
            for v in range(v0, v1):
                sent[k, v] = rows[:, (v - v0) * DS : (v - v0 + 1) * DS]
            raised(k, part).start()
        hand_on = jnp.logical_and(k == last, c != last)

        @pl.when(hand_on)
        def _():
            ahead(1, c).start()

        terms = dot(carried, coupled[lax.rem(k, 2), 0]).astype(BF16)

        @pl.when(hand_on)
        def _():
            for v in range(EARLY):
                base[v] = terms[:, v * DS : (v + 1) * DS]
            ahead(0, c).start()

        arrived(sk.at[k], sk_sem.at[k])
        tests = sk[k].T
        rank = jnp.sum(jnp.where(site_ids == k, ranks[...].astype(F32), 0.0), axis=1, keepdims=True)
        upper_rank = rank * bottom
        y0 = jnp.where(rows_f < rank, dot(tests, terms, NT), 0.0)

        @pl.when(k == 0)
        def _():
            for later in range(1, sites):
                pass_on(later)

        @pl.when(jnp.logical_and(k > 0, k + 1 < sites))
        def _():
            prepare(k + 1)

        for part in range(len(CUTS)):
            raised(k, part).wait_recv()
        lower = jnp.concatenate([below[k, v] for v in range(WB)], axis=1)
        y1 = jnp.where(rows_f < upper_rank, dot(tests, lower, NT), 0.0)
        y = jnp.concatenate([y0, y1], axis=1).astype(BF16)
        gram = dot(y, y, NT)
        ridge = jnp.where(rows_f < rank, DS / 4.0, 1.0)
        work[:, :DS] = gram + jnp.where(row_ids == column_ids, ridge, 0.0)
        work[:, DS:] = jnp.where(row_ids == column_ids, 1.0, 0.0)
        invert_factor(work, inverse)

        inv_high, inv_low = halves(inverse[...])
        frame = dot(jnp.concatenate([inv_high, inv_low], axis=1), jnp.concatenate([y, y], axis=0))
        plain[0, pl.ds(0, DS, stride=2), :] = frame[:, :DS]
        plain[0, pl.ds(1, DS, stride=2), :] = frame[:, DS:]
        iso[k] = plain[0].astype(BF16)
        deliver(k, 0)
        new = dot(frame.astype(BF16), jnp.concatenate([terms, lower], axis=0)).astype(BF16)
        for v in range(WB):
            car[k + 1, v] = new[:, v * DS : (v + 1) * DS]
        deliver(k, 1)

        @pl.when(k == 0)
        def _():
            prepare(1)

        return carry

    lax.fori_loop(0, sites, step, 0)

    for d in range(1, sites):
        for which in range(2):
            share(d, which).wait_send()
    for k in range(sites):
        for part in range(2):
            passed(k, part, blk.at[k, 0]).wait_send()
            raised(k, part).wait_send()

        @pl.when(c == k)
        def _():
            for which in range(2):
                kept(k, which).wait()

        @pl.when(c != k)
        def _():
            for which in range(2):
                (outgoing(k, which) if k < last else final(which, c)).wait_send()

    @pl.when(c != last)
    def _():
        for which in range(2):
            ahead(which, c).wait_send()
        for d in range(1, sites):
            peer = lax.rem(c + d, sites)
            to = {"chain": peer}
            remote(iso.at[0], sites_out.at[peer], o_send.at[0, 0], o_recv.at[peer, 0], to).wait_recv()
            remote(car.at[1], carry_out.at[peer], o_send.at[0, 1], o_recv.at[peer, 1], to).wait_recv()

    @pl.when(c == last)
    def _():
        placed = [
            (
                pltpu.make_async_copy(frames.at[a], sites_out.at[a], m_sem.at[a, 0]),
                pltpu.make_async_copy(made.at[a], carry_out.at[a, pl.ds(0, EARLY)], m_sem.at[a, 1]),
            )
            for a in range(last)
        ]
        for a in sorted(range(last), key=lambda a: min(last - a, a + 1)):
            ahead(0, a).wait_recv()
            ahead(1, a).wait_recv()
            final(0, a).wait_recv()
            placed[a][0].start()
            plain[0] = frames[a].astype(F32)
            frame = jnp.concatenate([plain[0, pl.ds(t, DS, stride=2), :] for t in range(2)], axis=1).astype(BF16)
            rows = jnp.concatenate(
                [jnp.concatenate([early[a, t, v] for v in range(EARLY)], axis=1) for t in range(2)], axis=0
            )
            new = dot(frame, rows).astype(BF16)
            for v in range(EARLY):
                made[a, v] = new[:, v * DS : (v + 1) * DS]
            placed[a][1].start()
        for a in range(last):
            final(1, a).wait_recv()
            for copy in placed[a]:
                copy.wait()


def keep(sites_in, carry_in, sites_out, carry_out, sem):
    copies = (
        pltpu.make_async_copy(carry_in, carry_out, sem.at[0]),
        pltpu.make_async_copy(sites_in, sites_out, sem.at[1]),
    )
    for copy in copies:
        copy.start()
    for copy in copies:
        copy.wait()


def per_device(site_blocks, left_carry, mpo, sketch, ranks):
    sites = lax.axis_size("chain")
    sectors = lax.axis_size("block")
    states = left_carry.shape[0]
    dma = pltpu.SemaphoreType.DMA
    vmem = pltpu.VMEM
    new_sites, carries = pl.pallas_call(
        functools.partial(kernel, sites, sectors),
        name="zip_up",
        out_shape=(
            jax.ShapeDtypeStruct((states, 2 * DS, DS), BF16),
            jax.ShapeDtypeStruct((states, WB, DS, DS), BF16),
        ),
        in_specs=[
            pl.BlockSpec(memory_space=pltpu.HBM),
            pl.BlockSpec(memory_space=pltpu.HBM),
            pl.BlockSpec(memory_space=pltpu.HBM),
            pl.BlockSpec(memory_space=pltpu.HBM),
            pl.BlockSpec(memory_space=pltpu.HBM),
        ],
        out_specs=(pl.BlockSpec(memory_space=pl.ANY), pl.BlockSpec(memory_space=pl.ANY)),
        scratch_shapes=[
            vmem(mpo.shape[:2] + (2, 2, WB), F32),
            vmem((1, sites), jnp.int32),
            vmem((sites, 3, 2 * DS, DS), BF16),
            vmem((sites, WB * DS, DS), BF16),
            vmem((sites + 1, WB, DS, DS), BF16),
            vmem((sites, WB, DS, DS), BF16),
            vmem((sites, WB, DS, DS), BF16),
            vmem((sites, 2 * DS, DS), BF16),
            vmem((2, 2, WB * DS, WB * DS), BF16),
            vmem((3, 2 * DS, DS), F32),
            vmem((DS, 2 * DS), F32),
            vmem((DS, DS), F32),
            vmem((EARLY, DS, DS), BF16),
            vmem((sites, 2, EARLY, DS, DS), BF16),
            vmem((sites, 2 * DS, DS), BF16),
            vmem((sites, EARLY, DS, DS), BF16),
            dma((2, sites)),
            dma((sites, 3)),
            dma((sites,)),
            dma((sites, 2)),
            dma((3,)),
            dma((sites, 2)),
            dma((sites, 2)),
            dma((sites, 2)),
            dma((sites, 2)),
            dma((2,)),
            dma((sites, 2)),
            dma((sites, 2)),
        ],
        compiler_params=pltpu.CompilerParams(
            collective_id=0, has_side_effects=True, vmem_limit_bytes=40 * 2**20
        ),
    )(*(pltpu.with_memory_space_constraint(x, pltpu.HBM) for x in (
        jnp.transpose(mpo, (0, 1, 3, 4, 2)),
        jnp.transpose(ranks),
        site_blocks.reshape(states, 2 * DS, DS),
        jnp.transpose(left_carry, (0, 2, 1, 3)),
        sketch.reshape(WB * DS, DS),
    )))
    new_sites, carries = pl.pallas_call(
        keep,
        name="keep",
        out_shape=(
            jax.ShapeDtypeStruct(new_sites.shape, BF16),
            jax.ShapeDtypeStruct(carries.shape, BF16),
        ),
        in_specs=[pl.BlockSpec(memory_space=pl.ANY)] * 2,
        out_specs=(pl.BlockSpec(memory_space=pltpu.HBM), pl.BlockSpec(memory_space=pltpu.HBM)),
        scratch_shapes=[dma((2,))],
        compiler_params=pltpu.CompilerParams(vmem_limit_bytes=2**20),
    )(new_sites, carries)
    return (
        new_sites.reshape(1, states, DS, 2, DS),
        jnp.transpose(carries, (0, 2, 1, 3))[None],
    )


def solution(mesh):
    return jax.shard_map(
        per_device,
        mesh=mesh,
        in_specs=(
            P("chain", None, "block", None, None),
            P(None, "block", None, None),
            P(),
            P("chain", "block", None, None),
            P(None, "block"),
        ),
        out_specs=(P("chain", None, "block", None, None), P("chain", None, "block", None, None)),
        check_vma=False,
    )
```
